32 devices in a mesh: member: 4 (over x, core), tile: 8 (over z, y).
Axes of the slice: x: 2, y: 2, z: 4, core: 2. Of those that a mesh axis runs over, the one named last changes fastest.
Arguments:
- state: bfloat16 [4, 8, 32, 32, 384], P('member', 'tile'), may hold values from -6 to 6
- cotangent: bfloat16 [4, 8, 32, 32, 384], P('member', 'tile'), may hold values from -6 to 6
- neighbors: int32 [8, 8], replicated, may hold values from -1 to 7, as said below
- kernel: float32 [7, 7, 384], replicated, may hold values from -0.875 to 0.875
- conv_bias: float32 [384], replicated, may hold values from -3 to 3
- norm_gain: float32 [384], replicated, may hold values from 0.25 to 1.75
- norm_shift: float32 [384], replicated, may hold values from -2 to 2
- w_in: bfloat16 [384, 1536], replicated, may hold values from -0.3125 to 0.3125
- bias_in: float32 [1536], replicated, may hold values from -3 to 3
- w_out: bfloat16 [1536, 384], replicated, may hold values from -0.15625 to 0.15625
- bias_out: float32 [384], replicated, may hold values from -3 to 3
- layer_scale: float32 [384], replicated, may hold values from 0.3 to 1
Outputs:
- new_state: bfloat16 [4, 8, 32, 32, 384], P('member', 'tile')
- state_grad: bfloat16 [4, 8, 32, 32, 384], P('member', 'tile')
- grad_w_in: float32 [384, 1536], P(None, 'tile')
- grad_w_out: float32 [1536, 384], P('tile')
- grad_kernel: float32 [7, 7, 384], replicated
- grad_bias_in: float32 [1536], replicated
- grad_channels: float32 [5, 384], replicated
The draws below stay inside these ranges and needn't reach their ends.
Inputs may be any that keep to these rules, and one draw needn't show every extreme that they name: Land tiles and tiles beyond the band's northern or southern edge are -1; longitude wraps around over 6 columns. If neighbors[t, d] = s then neighbors[s, opposite of d] = t. Wet tiles are numbered column by column, the columns of 2 tiles taken alternately upward and downward, so two neighbouring wet tiles differ in index by at most 3, counted cyclically over all wet tiles.
All inputs are finite; a program needn't handle non-finite values.
Results may differ from the reference program's by a relative error of at most 0.0062.
Values may be sent and summed in bfloat16 or wider, within the bound.
A program may use at most 128 MiB of HBM per device.

```python
import math
import jax
import jax.numpy as jnp
from jax import lax

C = 384
HID = 1536
KS = 7
TS = 32
GRID_Y = 2
GRID_X = 6
TILES = 8
MEMBERS = 4
N_TILE = 8


def draw_neighbors(key, part):
    cells = GRID_X * GRID_Y
    order = jax.random.permutation(key, cells - 2)
    wet_at = jnp.zeros((cells,), jnp.int32).at[order[:N_TILE - 2]].set(1)
    wet_at = wet_at.at[cells - 2].set(1).at[cells - 1].set(1)
    place = jnp.arange(cells, dtype=jnp.int32)
    column = place // GRID_Y
    within = place % GRID_Y
    row = jnp.where(column % 2 == 0, within, GRID_Y - 1 - within)
    cell_at = row * GRID_X + column
    rank = (jnp.cumsum(wet_at) - 1).astype(jnp.int32)
    index_of = jnp.full((cells,), -1, jnp.int32).at[cell_at].set(jnp.where(wet_at > 0, rank, -1))
    slot = jnp.where(wet_at > 0, rank, N_TILE)
    tile_cell = jnp.zeros((N_TILE,), jnp.int32).at[slot].set(cell_at, mode='drop')
    tile_x = tile_cell % GRID_X
    tile_y = tile_cell // GRID_X
    steps_x = jnp.array([0, 0, 1, -1, 1, -1, 1, -1], jnp.int32)
    steps_y = jnp.array([1, -1, 0, 0, 1, 1, -1, -1], jnp.int32)
    next_x = (tile_x[:, None] + steps_x[None, :]) % GRID_X
    next_y = tile_y[:, None] + steps_y[None, :]
    inside = (next_y >= 0) & (next_y < GRID_Y)
    looked = index_of[jnp.clip(next_y, 0, GRID_Y - 1) * GRID_X + next_x]
    return jnp.where(inside, looked, -1).astype(jnp.int32)


def block_scale(rng, dims, split, least, largest):
    loudness = 1.0
    for position, shards_of in split:
        heights = jax.random.uniform(jax.random.fold_in(jax.random.fold_in(rng, 6), position), (shards_of,), jnp.float32, least / len(split), largest / len(split))
        loudness = loudness * jnp.repeat(jnp.exp(heights), dims[position] // shards_of).reshape((-1,) + (1,) * (len(dims) - 1 - position))
    return loudness


def bell_draw(own_key, dims, scale, reach, shards=(), kind=jnp.bfloat16):
    drawn = scale * jax.random.normal(own_key, dims, jnp.float32)
    if shards:
        drawn = drawn * block_scale(own_key, dims, shards, -0.22, 0.18)
    return jnp.clip(drawn, -reach, reach).astype(kind)


def setup_inputs(seed: int = 0) -> dict:
    arg_keys = jax.random.split(jax.random.key(seed), 13)
    return {
        "state": bell_draw(arg_keys[0], (MEMBERS, TILES, TS, TS, C), 1.0, 6.0, ((0, 4), (1, 8))),
        "cotangent": bell_draw(arg_keys[1], (MEMBERS, TILES, TS, TS, C), 1.0, 6.0, ((0, 4), (1, 8))),
        "neighbors": draw_neighbors(jax.random.fold_in(arg_keys[12], 71), 0),
        "kernel": bell_draw(arg_keys[3], (KS, KS, C), (KS * KS) ** -0.5, 0.875, (), jnp.float32),
        "conv_bias": bell_draw(arg_keys[4], (C,), 0.5, 3.0, (), jnp.float32),
        "norm_gain": jnp.clip(1.0 + 0.15 * jax.random.normal(arg_keys[5], (C,), jnp.float32), 0.25, 1.75),
        "norm_shift": bell_draw(arg_keys[6], (C,), 0.3, 2.0, (), jnp.float32),
        "w_in": bell_draw(arg_keys[7], (C, HID), C ** -0.5, 0.3125),
        "bias_in": bell_draw(arg_keys[8], (HID,), 0.5, 3.0, (), jnp.float32),
        "w_out": bell_draw(arg_keys[9], (HID, C), HID ** -0.5, 0.15625),
        "bias_out": bell_draw(arg_keys[10], (C,), 0.5, 3.0, (), jnp.float32),
        "layer_scale": jnp.clip(jnp.exp(jax.random.uniform(arg_keys[11], (C,), jnp.float32, math.log(0.3), math.log(1.0))), 0.3, 1.0),
    }


GELU_SCALE = 0.7978845608028654
GELU_CUBIC = 0.044715
EPSILON = 1e-06

def contract_rows(left, right):
    return lax.dot_general(left, right, (((0,), (0,)), ((), ())), preferred_element_type=jnp.float32)

def contract_cols(left, right):
    return lax.dot_general(left, right, (((1,), (1,)), ((), ())), preferred_element_type=jnp.float32)

def framed(center, north, south, east, west, north_east, north_west, south_east, south_west):
    lower = jnp.concatenate([south_west, south, south_east], axis=1)
    middle = jnp.concatenate([west, center, east], axis=1)
    upper = jnp.concatenate([north_west, north, north_east], axis=1)
    return jnp.concatenate([lower, middle, upper], axis=0)

def fetch(tiles, index):
    tile = tiles[jnp.maximum(index, 0)]
    return jnp.where(index >= 0, tile, jnp.zeros_like(tile))

def frame_from(tiles, links, center, margin):
    side = center.shape[0]
    edge = side - margin
    got = [fetch(tiles, links[way]) for way in range(8)]
    return framed(center, got[0][:margin], got[1][edge:], got[2][:, :margin], got[3][:, edge:], got[4][:margin, :margin], got[5][:margin, edge:], got[6][edge:, :margin], got[7][edge:, edge:])

def depthwise(padded, kernel):
    taps = kernel.shape[0]
    side = padded.shape[0] - taps + 1
    total = jnp.zeros((side, side, padded.shape[2]), jnp.float32)
    for row_off in range(taps):
        for col_off in range(taps):
            total = total + kernel[row_off, col_off] * padded[row_off:row_off + side, col_off:col_off + side].astype(jnp.float32)
    return total

def transposed(padded, kernel):
    taps = kernel.shape[0]
    side = padded.shape[0] - taps + 1
    total = jnp.zeros((side, side, padded.shape[2]), jnp.float32)
    for row_off in range(taps):
        for col_off in range(taps):
            row_at = taps - 1 - row_off
            col_at = taps - 1 - col_off
            total = total + kernel[row_off, col_off] * padded[row_at:row_at + side, col_at:col_at + side].astype(jnp.float32)
    return total

def kernel_grad(padded, grad_mixed):
    taps = padded.shape[0] - grad_mixed.shape[0] + 1
    side = grad_mixed.shape[0]
    rows = []
    for row_off in range(taps):
        line = []
        for col_off in range(taps):
            window = padded[row_off:row_off + side, col_off:col_off + side].astype(jnp.float32)
            line.append(lax.optimization_barrier(jnp.sum(window * grad_mixed, axis=(0, 1))))
        rows.append(jnp.stack(line))
    return jnp.stack(rows)

def forward_backward(padded, center, cot_tile, kernel, conv_bias, norm_gain, norm_shift, w_in, bias_in, w_out, bias_out, layer_scale):
    side, width = (center.shape[0], center.shape[2])
    mixed = (depthwise(padded, kernel) + conv_bias).reshape(side * side, width)
    centered = mixed - lax.optimization_barrier(jnp.mean(mixed, axis=1, keepdims=True))
    variance = lax.optimization_barrier(jnp.mean(centered * centered, axis=1, keepdims=True))
    inv_std = lax.rsqrt(variance + EPSILON)
    norm_hat = centered * inv_std
    normed = (norm_hat * norm_gain + norm_shift).astype(jnp.bfloat16)
    pre_act = jnp.dot(normed, w_in, preferred_element_type=jnp.float32) + bias_in
    tanh_value = jnp.tanh(GELU_SCALE * (pre_act + GELU_CUBIC * pre_act * pre_act * pre_act))
    activation = (0.5 * pre_act * (1.0 + tanh_value)).astype(jnp.bfloat16)
    branch = jnp.dot(activation, w_out, preferred_element_type=jnp.float32) + bias_out
    flat_state = center.reshape(side * side, width).astype(jnp.float32)
    new_tile = (flat_state + layer_scale * branch).astype(jnp.bfloat16).reshape(side, side, width)
    flat_cot = cot_tile.reshape(side * side, width).astype(jnp.float32)
    grad_branch = layer_scale * flat_cot
    branch_low = grad_branch.astype(jnp.bfloat16)
    grad_wout = contract_rows(activation, branch_low)
    grad_bout = lax.optimization_barrier(jnp.sum(grad_branch, axis=0))
    grad_gamma = lax.optimization_barrier(jnp.sum(flat_cot * branch, axis=0))
    grad_act = contract_cols(branch_low, w_out)
    slope = 0.5 * (1.0 + tanh_value) + 0.5 * pre_act * (1.0 - tanh_value * tanh_value) * GELU_SCALE * (1.0 + 3.0 * GELU_CUBIC * pre_act * pre_act)
    grad_pre = grad_act * slope
    grad_pre_b = grad_pre.astype(jnp.bfloat16)
    grad_win = contract_rows(normed, grad_pre_b)
    grad_bin = lax.optimization_barrier(jnp.sum(grad_pre, axis=0))
    grad_normed = contract_cols(grad_pre_b, w_in)
    grad_gain = lax.optimization_barrier(jnp.sum(grad_normed * norm_hat, axis=0))
    grad_shift = lax.optimization_barrier(jnp.sum(grad_normed, axis=0))
    scaled = grad_normed * norm_gain
    grad_mixed = inv_std * (scaled - lax.optimization_barrier(jnp.mean(scaled, axis=1, keepdims=True)) - norm_hat * lax.optimization_barrier(jnp.mean(scaled * norm_hat, axis=1, keepdims=True)))
    grad_mixed = grad_mixed.reshape(side, side, width)
    grad_kern = kernel_grad(padded, grad_mixed)
    grad_conv = lax.optimization_barrier(jnp.sum(grad_mixed, axis=(0, 1)))
    grads = (grad_win, grad_wout, grad_kern, grad_bin, grad_conv, grad_gain, grad_shift, grad_bout, grad_gamma)
    return (new_tile, grad_mixed.astype(jnp.bfloat16), grads)

def reference(state, cotangent, neighbors, kernel, conv_bias, norm_gain, norm_shift, w_in, bias_in, w_out, bias_out, layer_scale):
    members, count, side, width = (state.shape[0], state.shape[1], state.shape[2], state.shape[4])
    hidden = w_in.shape[1]
    taps = kernel.shape[0]
    margin = taps // 2

    def first(totals, index):
        member = index // count
        tile = index % count
        tiles = state[member]
        center = tiles[tile]
        padded = frame_from(tiles, neighbors[tile], center, margin)
        new_tile, grad_low, grads = forward_backward(padded, center, cotangent[member, tile], kernel, conv_bias, norm_gain, norm_shift, w_in, bias_in, w_out, bias_out, layer_scale)
        totals = tuple((total + term for total, term in zip(totals, grads)))
        return (totals, (new_tile, grad_low))
    zeros_c = jnp.zeros((width,), jnp.float32)
    start = (jnp.zeros((width, hidden), jnp.float32), jnp.zeros((hidden, width), jnp.float32), jnp.zeros((taps, taps, width), jnp.float32), jnp.zeros((hidden,), jnp.float32), zeros_c, zeros_c, zeros_c, zeros_c, zeros_c)
    totals, (news, grad_lows) = lax.scan(first, start, jnp.arange(members * count, dtype=jnp.int32))
    grad_lows = grad_lows.reshape(members, count, side, side, width)

    def second(index):
        member = index // count
        tile = index % count
        tiles = grad_lows[member]
        padded = frame_from(tiles, neighbors[tile], tiles[tile], margin)
        back = transposed(padded, kernel)
        return (cotangent[member, tile].astype(jnp.float32) + back).astype(jnp.bfloat16)
    state_grad = lax.map(second, jnp.arange(members * count, dtype=jnp.int32)).reshape(members, count, side, side, width)
    new_state = news.reshape(members, count, side, side, width)
    factor = 1.0 / math.sqrt(members * count * side * side)
    grad_win, grad_wout, grad_kern, grad_bin, grad_conv, grad_gain, grad_shift, grad_bout, grad_gamma = totals
    channels = jnp.stack([grad_conv, grad_gain, grad_shift, grad_bout, grad_gamma]) * factor
    return (new_state, state_grad, grad_win * factor, grad_wout * factor, grad_kern * factor, grad_bin * factor, channels)
```

```python
import functools
import math

import jax
import jax.numpy as jnp
from jax import lax
from jax.experimental import pallas as pl
from jax.experimental.pallas import tpu as pltpu
from jax.sharding import PartitionSpec as P

OFFSETS = (1, 2, 3, -1, -2, -3)
GELU_SCALE = 0.7978845608028654
GELU_CUBIC = 0.044715
EPSILON = 1e-06
LANES = 128
LEAD = 8
MESH = pl.DeviceIdType.MESH
F32 = jnp.float32
BF16 = jnp.bfloat16
VMEM_LIMIT = 56 << 20


def vmem_spec():
    return pl.BlockSpec(memory_space=pltpu.VMEM)


def smem_spec():
    return pl.BlockSpec(memory_space=pltpu.SMEM)


def local_params():
    return pltpu.CompilerParams(vmem_limit_bytes=VMEM_LIMIT)


def remote_params(ident):
    return pltpu.CompilerParams(
        collective_id=ident, has_side_effects=True, vmem_limit_bytes=VMEM_LIMIT
    )


def pitch_of(side):
    return side + 2 * LEAD


def spread_of(side, margin):
    return (side + 2 * margin) * pitch_of(side)


def place(padded, side, margin, center):
    pitch = pitch_of(side)
    for part in range(padded.shape[0]):

        def clear(row, carry):
            at = pl.ds(pl.multiple_of(row * pitch, 8), pitch)
            padded[part, at, :] = jnp.zeros((pitch, LANES), F32)
            return carry

        lax.fori_loop(0, side + 2 * margin, clear, 0)

        def put(row, carry):
            at = pl.ds(pl.multiple_of((margin + row) * pitch + LEAD, 8), side)
            padded[part, at, :] = center(part, row)
            return carry

        lax.fori_loop(0, side, put, 0)


def around(tile, count):
    takers = [lax.rem(tile + offset + count, count) for offset in OFFSETS]
    givers = [lax.rem(tile - offset + count, count) for offset in OFFSETS]
    return takers, givers


def pack(padded, side, margin, want, send_ref):
    pitch = pitch_of(side)
    edge = side - margin
    for part in range(padded.shape[0]):
        lanes = pl.ds(part * LANES, LANES)
        for k in range(margin):
            low = (margin + k) * pitch + LEAD
            high = (margin + edge + k) * pitch + LEAD
            first = margin * pitch + LEAD
            lines = [
                padded[part, pl.ds(low, side), :],
                padded[part, pl.ds(high, side), :],
                padded[part, pl.ds(first + k, side, stride=pitch), :],
                padded[part, pl.ds(first + edge + k, side, stride=pitch), :],
            ]
            lines = lines + [
                jnp.concatenate([lines[0][:8]] * (side // 8), axis=0),
                jnp.concatenate([lines[0][side - 8 :]] * (side // 8), axis=0),
                jnp.concatenate([lines[1][:8]] * (side // 8), axis=0),
                jnp.concatenate([lines[1][side - 8 :]] * (side // 8), axis=0),
            ]
            for slot in range(len(OFFSETS)):
                line = lines[7]
                for way in range(7):
                    line = jnp.where(want[slot][way], lines[way], line)
                send_ref[slot, k, :, lanes] = line.astype(BF16)


def unpack(padded, side, margin, have, recv_ref):
    pitch = pitch_of(side)
    for part in range(padded.shape[0]):
        lanes = pl.ds(part * LANES, LANES)
        for k in range(margin):
            lines = [recv_ref[slot, k, :, lanes].astype(F32) for slot in range(len(OFFSETS))]
            for way in range(8):
                size = side if way < 4 else 8
                line = jnp.zeros((size, LANES), F32)
                for slot in range(len(OFFSETS)):
                    line = jnp.where(have[slot][way], lines[slot][:size], line)
                if way == 0:
                    at = pl.ds((margin + side + k) * pitch + LEAD, side)
                elif way == 1:
                    at = pl.ds(k * pitch + LEAD, side)
                elif way == 2:
                    at = pl.ds(margin * pitch + LEAD + side + k, side, stride=pitch)
                elif way == 3:
                    at = pl.ds(margin * pitch + LEAD - margin + k, side, stride=pitch)
                else:
                    row = margin + side + k if way in (4, 5) else k
                    at = pl.ds(row * pitch + (LEAD + side if way in (4, 6) else LEAD - 8), 8)
                padded[part, at, :] = line


def convolve(padded, part, kern_ref, side, taps, flipped, emit, group=4, first=0, gap=1, steps=None):
    pitch = pitch_of(side)
    margin = taps // 2
    lanes = pl.ds(part * LANES, LANES)

    def step(index, carry):
        base = (first + index * gap) * group
        total = [jnp.zeros((side, LANES), F32) for _ in range(group)]
        for col in range(taps):
            for row in range(group + taps - 1):
                start = (base + row) * pitch
                line = padded[part, pl.ds(start + (LEAD - margin + col), side), :]
                for out in range(group):
                    up = row - out
                    if 0 <= up < taps:
                        a, b = (taps - 1 - up, taps - 1 - col) if flipped else (up, col)
                        total[out] = total[out] + kern_ref[a, pl.ds(b, 1), lanes] * line
        for out in range(group):
            emit(pl.multiple_of((base + out) * side, side), total[out])
        return carry

    lax.fori_loop(0, side // group if steps is None else steps, step, 0)


def edge_columns(sides, part, kern_ref, side, taps, add, group=4):
    margin = taps // 2
    lanes = pl.ds(part * LANES, LANES)

    def step(index, carry):
        base = (1 + index) * group
        for east in range(2):
            total = [jnp.zeros((8, LANES), F32) for _ in range(group)]
            for near in range(margin):
                col = margin + 1 + near if east else near
                shift = 1 + near if east else 8 - margin + near
                for row in range(group + taps - 1):
                    line = sides[east, part, pl.ds((base + row) * 16 + shift, 8), :]
                    for out in range(group):
                        up = row - out
                        if 0 <= up < taps:
                            total[out] = total[out] + kern_ref[up, pl.ds(col, 1), lanes] * line
            for out in range(group):
                start = (base + out) * side + (side - 8 if east else 0)
                add(pl.multiple_of(start, 8), total[out])
        return carry

    lax.fori_loop(0, side // group - 2, step, 0)


def kernel_grad(padded, part, grad_ref, side, taps, emit, group=4):
    pitch = pitch_of(side)
    margin = taps // 2
    for col in range(taps):

        def step(index, sums):
            sums = list(sums)
            base = index * group
            grads = [
                grad_ref[part, pl.ds(pl.multiple_of((base + out) * side, side), side), :]
                for out in range(group)
            ]
            for row in range(group + taps - 1):
                start = (base + row) * pitch
                line = padded[part, pl.ds(start + (LEAD - margin + col), side), :]
                for out in range(group):
                    up = row - out
                    if 0 <= up < taps:
                        product = line * grads[out]
                        for piece in range(side // 8):
                            sums[up] = sums[up] + product[piece * 8 : piece * 8 + 8]
            return tuple(sums)

        zero = jnp.zeros((8, LANES), F32)
        sums = lax.fori_loop(0, side // group, step, (zero,) * taps)
        for up in range(taps):
            emit(up, col, jnp.sum(sums[up], axis=0, keepdims=True))


def prepare(source, target, sems, slot, **device):
    return pltpu.make_async_remote_copy(
        src_ref=source,
        dst_ref=target,
        send_sem=sems.at[0, slot],
        recv_sem=sems.at[1, slot],
        device_id=device,
        device_id_type=MESH,
    )


def remote(source, target, sems, slot, **device):
    copy = prepare(source, target, sems, slot, **device)
    copy.start()
    return copy


def swap_halo(padded, side, margin, links_ref, send_ref, recv_ref, sems, count, ready):
    tile = lax.axis_index("tile")
    takers, _ = around(tile, count)
    want = [[links_ref[taker, way] == tile for way in range(8)] for taker in takers]
    pack(padded, side, margin, want, send_ref)
    ready()
    return [
        remote(send_ref.at[slot], recv_ref.at[slot], sems, slot, tile=taker)
        for slot, taker in enumerate(takers)
    ]


def take_halo(padded, side, margin, links_ref, recv_ref, count):
    tile = lax.axis_index("tile")
    _, givers = around(tile, count)
    have = [[links_ref[tile, way] == giver for way in range(8)] for giver in givers]
    unpack(padded, side, margin, have, recv_ref)


def contract_rows(left, right):
    return lax.dot_general(left, right, (((0,), (0,)), ((), ())), preferred_element_type=F32)


def contract_cols(left, right):
    return lax.dot_general(left, right, (((1,), (1,)), ((), ())), preferred_element_type=F32)


def whole_kernel(
    side,
    taps,
    members,
    tiles,
    chunk,
    block,
    links_ref,
    state_ref,
    kern_ref,
    cbias_ref,
    gain_ref,
    shift_ref,
    bin_ref,
    bout_ref,
    scale_ref,
    cot_hbm,
    win_hbm,
    wout_hbm,
    new_hbm,
    sgrad_hbm,
    out_ref,
    sout_ref,
    padded,
    gpad,
    sides,
    mixed_ref,
    inv_ref,
    normed_ref,
    low_ref,
    act_ref,
    glow_ref,
    branch_ref,
    gnorm_ref,
    gmix_ref,
    gbin_ref,
    gch_ref,
    cot_ref,
    win_ref,
    wout_ref,
    new_ref,
    sgrad_ref,
    send,
    recv,
    gsend,
    grecv,
    big,
    core_in,
    x_out,
    x_in,
    t_out,
    t_in,
    own,
    s_pack,
    sm_in,
    st_out,
    st_in,
    s_own,
    load_sem,
    halo_sem,
    ghalo_sem,
    core_sem,
    x_sem,
    t_send,
    t_recv,
    g_sem,
    sm_sem,
    st_sem,
    sg_sem,
    store_sem,
):
    margin = taps // 2
    parts = padded.shape[0]
    cells = side * side
    groups = side // 4
    pitch = pitch_of(side)
    hidden = win_ref.shape[1]
    width = win_ref.shape[0]
    chunks = hidden // chunk
    per = tiles // chunks
    spots = members // 2
    rows = hidden // (tiles * members)
    member = lax.axis_index("member")
    tile = lax.axis_index("tile")
    core = lax.rem(member, 2)
    cross = member // 2
    mates = [lax.rem(member + k, members) for k in range(1, members)]
    peers = [lax.rem(tile + k, tiles) for k in range(1, tiles)]
    barrier = pltpu.get_barrier_semaphore()
    for mate in mates:
        pl.semaphore_signal(barrier, inc=1, device_id={"member": mate}, device_id_type=MESH)
    for peer in peers:
        pl.semaphore_signal(barrier, inc=1, device_id={"tile": peer}, device_id_type=MESH)
    loads = [
        pltpu.make_async_copy(source, target, load_sem.at[k])
        for k, (source, target) in enumerate(
            [(cot_hbm, cot_ref), (win_hbm, win_ref), (wout_hbm, wout_ref)]
        )
    ]
    for load in loads:
        load.start()

    def center(part, row):
        at = pl.ds(pl.multiple_of(row * side, side), side)
        return state_ref[at, pl.ds(part * LANES, LANES)].astype(F32)

    place(padded, side, margin, center)
    halo = swap_halo(
        padded, side, margin, links_ref, send, recv, halo_sem, tiles,
        lambda: pl.semaphore_wait(barrier, members + tiles - 2),
    )

    def make_emit(part):
        lanes = pl.ds(part * LANES, LANES)
        bias = cbias_ref[lanes].reshape(1, LANES)

        def emit(start, value):
            mixed_ref[pl.ds(start, side), lanes] = value + bias

        return emit

    for part in range(parts):
        convolve(
            padded, part, kern_ref, side, taps, False, make_emit(part), first=1, steps=groups - 2
        )
    for copy in halo:
        copy.wait()
    take_halo(padded, side, margin, links_ref, recv, tiles)
    for part in range(parts):
        lanes = pl.ds(part * LANES, LANES)

        def frame(row, carry):
            at = pl.ds(pl.multiple_of(row * 16, 8), 8)
            after = pl.ds(pl.multiple_of(row * 16 + 8, 8), 8)
            start = row * pitch + LEAD
            blank = jnp.zeros((8, LANES), F32)
            sides[0, part, at, :] = padded[part, pl.ds(pl.multiple_of(start - 8, 8), 8), :]
            sides[0, part, after, :] = blank
            sides[1, part, at, :] = blank
            sides[1, part, after, :] = padded[part, pl.ds(pl.multiple_of(start + side, 8), 8), :]
            return carry

        lax.fori_loop(0, side + 2 * margin, frame, 0)

        def add(start, value):
            mixed_ref[pl.ds(start, 8), lanes] += value

        convolve(
            padded, part, kern_ref, side, taps, False, make_emit(part), gap=groups - 1, steps=2
        )
        edge_columns(sides, part, kern_ref, side, taps, add)

    gbin_ref[...] = jnp.zeros_like(gbin_ref)
    gch_ref[...] = jnp.zeros_like(gch_ref)
    for load in loads:
        load.wait()

    def prepare_cells(at):
        mixed = mixed_ref[at, :]
        centered = mixed - jnp.mean(mixed, axis=1, keepdims=True)
        variance = jnp.mean(centered * centered, axis=1, keepdims=True)
        inv_std = lax.rsqrt(variance + EPSILON)
        norm_hat = centered * inv_std
        mixed_ref[at, :] = norm_hat
        inv_ref[at, :] = jnp.broadcast_to(inv_std, (block, LANES))
        normed_ref[at, :] = (norm_hat * gain_ref[...].reshape(1, -1) + shift_ref[...].reshape(1, -1)).astype(BF16)
        grad_branch = scale_ref[...].reshape(1, -1) * cot_ref[at, :].astype(F32)
        low_ref[at, :] = grad_branch.astype(BF16)
        gch_ref[3:4, :] += jnp.sum(grad_branch, axis=0, keepdims=True)

    def finish_cells(at, branch, grad_normed):
        gain = gain_ref[...].reshape(1, -1)
        branch = branch + bout_ref[...].reshape(1, -1)
        scaled_branch = scale_ref[...].reshape(1, -1) * branch
        new_ref[at, :] = (state_ref[at, :].astype(F32) + scaled_branch).astype(BF16)
        norm_hat = mixed_ref[at, :]
        scaled = grad_normed * gain
        inner = (
            scaled
            - jnp.mean(scaled, axis=1, keepdims=True)
            - norm_hat * jnp.mean(scaled * norm_hat, axis=1, keepdims=True)
        )
        inv_std = inv_ref[at, :]
        for part in range(parts):
            lanes = slice(part * LANES, (part + 1) * LANES)
            grad_mixed = inv_std * inner[:, lanes]
            gmix_ref[part, at, :] = grad_mixed
            gch_ref[0:1, lanes] += jnp.sum(grad_mixed, axis=0, keepdims=True)
        gch_ref[1:2, :] += jnp.sum(grad_normed * norm_hat, axis=0, keepdims=True)
        gch_ref[2:3, :] += jnp.sum(grad_normed, axis=0, keepdims=True)
        gch_ref[4:5, :] += jnp.sum(cot_ref[at, :].astype(F32) * branch, axis=0, keepdims=True)

    def cross_pair(h):
        return prepare(
            big.at[h, :, :, :, 1 - core], core_in.at[h], core_sem, h, member=cross * 2 + 1 - core
        )

    def cross_over(h):
        copies = []
        for k in range(1, spots):
            spot = lax.rem(cross + k, spots)
            copies.append(
                prepare(
                    x_out.at[h, spot], x_in.at[h, k - 1], x_sem, h * (spots - 1) + k - 1,
                    member=spot * 2 + core,
                )
            )
        return copies

    def start_cross_over(h):
        cross_pair(h).wait()

        def add(t, carry):
            for kind in range(2):
                for x in range(spots):
                    mine = big[h, kind, t, x, core].astype(F32)
                    x_out[h, x, kind, t] = (mine + core_in[h, kind, t, x].astype(F32)).astype(BF16)
            return carry

        lax.fori_loop(0, per, add, 0)
        for copy in cross_over(h):
            copy.start()

    def along(h, k):
        peer = peers[k]
        spot = jnp.clip(peer - h * per, 0, per - 1)
        return pltpu.make_async_remote_copy(
            src_ref=t_out.at[h, spot],
            dst_ref=t_in.at[k],
            send_sem=t_send.at[h, k],
            recv_sem=t_recv.at[k],
            device_id={"tile": peer},
            device_id_type=MESH,
        )

    def start_along(h):
        for copy in cross_over(h):
            copy.wait()

        def add(t, carry):
            for kind in range(2):
                value = x_out[h, cross, kind, t].astype(F32)
                for k in range(spots - 1):
                    value = value + x_in[h, k, kind, t].astype(F32)
                t_out[h, t, kind] = value.astype(BF16)
            return carry

        lax.fori_loop(0, per, add, 0)
        for k in range(tiles - 1):

            @pl.when(peers[k] // per == h)
            def _():
                along(h, k).start()

    def mlp(h, r):
        at = pl.ds(pl.multiple_of(r * block, block), block)
        if h == 0:
            prepare_cells(at)
        here = slice(h * chunk, (h + 1) * chunk)
        win = win_ref[:, here]
        wout = wout_ref[here, :]
        pre = jnp.dot(normed_ref[at, :], win, preferred_element_type=F32) + bin_ref[
            pl.ds(h * chunk, chunk)
        ].reshape(1, chunk)
        square = pre * pre
        tanh_value = jnp.tanh(GELU_SCALE * pre * (1.0 + GELU_CUBIC * square))
        half = 0.5 * (1.0 + tanh_value)
        activation = (pre * half).astype(BF16)
        slope = half + (0.5 * GELU_SCALE) * pre * (1.0 - tanh_value * tanh_value) * (
            1.0 + 3.0 * GELU_CUBIC * square
        )
        grad_pre = contract_cols(low_ref[at, :], wout) * slope
        grad_low = grad_pre.astype(BF16)
        act_ref[at, :] = activation
        glow_ref[at, :] = grad_low
        gbin_ref[:, here] += jnp.sum(grad_pre, axis=0, keepdims=True)
        branch = jnp.dot(activation, wout, preferred_element_type=F32)
        grad_normed = contract_cols(grad_low, win)
        if h > 0:
            branch = branch_ref[at, :] + branch
            grad_normed = gnorm_ref[at, :] + grad_normed
        if h < chunks - 1:
            branch_ref[at, :] = branch
            gnorm_ref[at, :] = grad_normed
        else:
            finish_cells(at, branch, grad_normed)

    def weights(h):
        for kind, (left, right) in enumerate([(glow_ref, normed_ref), (act_ref, low_ref)]):
            value = contract_rows(left[...], right[...])
            for index in range(per * members):
                t, x, c = index // members, index % members // 2, index % 2
                big[h, kind, t, x, c] = value[index * rows : (index + 1) * rows].astype(BF16)
        cross_pair(h).start()

    for h in range(chunks):

        def step(r, carry):
            mlp(h, r)
            if h == chunks - 1 and chunks > 1:

                @pl.when(r == 0)
                def _():
                    start_cross_over(0)

            return carry

        lax.fori_loop(0, cells // block, step, 0)
        if h < chunks - 1:
            weights(h)

    new_copy = pltpu.make_async_copy(new_ref, new_hbm, store_sem.at[0])
    new_copy.start()

    def gcenter(part, row):
        at = pl.ds(pl.multiple_of(row * side, side), side)
        return gmix_ref[part, at, :].astype(BF16).astype(F32)

    place(gpad, side, margin, gcenter)
    ghalo = swap_halo(
        gpad, side, margin, links_ref, gsend, grecv, ghalo_sem, tiles, lambda: None
    )
    weights(chunks - 1)
    if chunks > 1:
        start_along(0)

    lines = s_pack.shape[1]
    s_pack[...] = jnp.zeros_like(s_pack)
    first = taps * taps
    extra = gbin_ref.shape[1] // width
    for row in range(extra):
        at = first + row
        s_pack[at // lines, pl.ds(at % lines, 1), :] = gbin_ref[:, pl.ds(row * width, width)]
    for row in range(5):
        at = first + extra + row
        s_pack[at // lines, pl.ds(at % lines, 1), :] = gch_ref[pl.ds(row, 1), :]

    def own_kernel(part):
        def emit(up, col, value):
            at = up * taps + col
            s_pack[at // lines, pl.ds(at % lines, 1), pl.ds(part * LANES, LANES)] = value

        kernel_grad(padded, part, gmix_ref, side, taps, emit)

    def conv(part):
        lanes = pl.ds(part * LANES, LANES)

        def emit(start, value):
            at = pl.ds(start, side)
            sgrad_ref[at, lanes] = (cot_ref[at, lanes].astype(F32) + value).astype(BF16)

        convolve(gpad, part, kern_ref, side, taps, True, emit)

    own_kernel(0)
    start_cross_over(chunks - 1)
    for part in range(1, parts):
        own_kernel(part)
    small = [remote(s_pack, sm_in.at[k], sm_sem, k, member=mate) for k, mate in enumerate(mates)]
    start_along(chunks - 1)
    for copy in ghalo:
        copy.wait()
    take_halo(gpad, side, margin, links_ref, grecv, tiles)
    conv(0)
    for copy in small:
        copy.wait()
    total = s_pack[...]
    for k in range(members - 1):
        total = total + sm_in[k]
    st_out[...] = total
    small = [
        remote(st_out.at[peer], st_in.at[k], st_sem, k, tile=peer) for k, peer in enumerate(peers)
    ]
    conv(1)
    for k in range(tiles - 1):
        along(0, k).wait_recv()
        for h in range(chunks):

            @pl.when(peers[k] // per == h)
            def _():
                along(h, k).wait_send()

    for h in range(chunks):

        @pl.when(tile // per == h)
        def _():
            for kind in range(2):
                value = t_out[h, tile - h * per, kind].astype(F32)
                for k in range(tiles - 1):
                    value = value + t_in[k, kind].astype(F32)
                own[kind] = value.astype(BF16)

    out_ref[member] = own[...]
    back = [
        remote(own, out_ref.at[member], g_sem, k, member=mate) for k, mate in enumerate(mates)
    ]
    for copy in small:
        copy.wait()
    total = st_out[tile]
    for k in range(tiles - 1):
        total = total + st_in[k]
    s_own[...] = total
    sout_ref[tile] = total
    small = [
        remote(s_own, sout_ref.at[tile], sg_sem, k, tile=peer) for k, peer in enumerate(peers)
    ]
    for part in range(2, parts):
        conv(part)
    store = pltpu.make_async_copy(sgrad_ref, sgrad_hbm, store_sem.at[1])
    store.start()
    for copy in small + back:
        copy.wait()
    new_copy.wait()
    store.wait()


def run_whole(links, state, cot, kern, vectors, w_in, w_out, side, members, tiles, chunk=768, block=512):
    cells, width = state.shape
    hidden = w_in.shape[1]
    taps = kern.shape[0]
    margin = taps // 2
    chunks = hidden // chunk
    per = tiles // chunks
    spots = members // 2
    rows = hidden // (tiles * members)
    used = taps * taps + hidden // width + 5
    lines = 8 * (-(-used // (8 * tiles)))
    others = max(spots - 1, 1)
    parts = width // LANES
    spread = spread_of(side, margin)
    dma = lambda *n: pltpu.SemaphoreType.DMA(n)
    strips = (len(OFFSETS), margin, side, width)
    anywhere = pl.BlockSpec(memory_space=pl.ANY)
    return pl.pallas_call(
        functools.partial(whole_kernel, side, taps, members, tiles, chunk, block),
        in_specs=[smem_spec()] + [vmem_spec()] * 8 + [anywhere] * 3,
        out_specs=[anywhere] * 2 + [vmem_spec()] * 2,
        out_shape=[
            jax.ShapeDtypeStruct((cells, width), BF16),
            jax.ShapeDtypeStruct((cells, width), BF16),
            jax.ShapeDtypeStruct((members, 2, rows, width), BF16),
            jax.ShapeDtypeStruct((tiles, lines, width), F32),
        ],
        scratch_shapes=[
            pltpu.VMEM((parts, spread, LANES), F32),
            pltpu.VMEM((parts, spread, LANES), F32),
            pltpu.VMEM((2, parts, (side + 2 * margin) * 16, LANES), F32),
            pltpu.VMEM((cells, width), F32),
            pltpu.VMEM((cells, LANES), F32),
            pltpu.VMEM((cells, width), BF16),
            pltpu.VMEM((cells, width), BF16),
            pltpu.VMEM((cells, chunk), BF16),
            pltpu.VMEM((cells, chunk), BF16),
            pltpu.VMEM((cells, width), F32),
            pltpu.VMEM((cells, width), F32),
            pltpu.VMEM((parts, cells, LANES), F32),
            pltpu.VMEM((1, hidden), F32),
            pltpu.VMEM((8, width), F32),
            pltpu.VMEM((cells, width), BF16),
            pltpu.VMEM((width, hidden), BF16),
            pltpu.VMEM((hidden, width), BF16),
            pltpu.VMEM((cells, width), BF16),
            pltpu.VMEM((cells, width), BF16),
            pltpu.VMEM(strips, BF16),
            pltpu.VMEM(strips, BF16),
            pltpu.VMEM(strips, BF16),
            pltpu.VMEM(strips, BF16),
            pltpu.VMEM((chunks, 2, per, spots, 2, rows, width), BF16),
            pltpu.VMEM((chunks, 2, per, spots, rows, width), BF16),
            pltpu.VMEM((chunks, spots, 2, per, rows, width), BF16),
            pltpu.VMEM((chunks, others, 2, per, rows, width), BF16),
            pltpu.VMEM((chunks, per, 2, rows, width), BF16),
            pltpu.VMEM((tiles - 1, 2, rows, width), BF16),
            pltpu.VMEM((2, rows, width), BF16),
            pltpu.VMEM((tiles, lines, width), F32),
            pltpu.VMEM((members - 1, tiles, lines, width), F32),
            pltpu.VMEM((tiles, lines, width), F32),
            pltpu.VMEM((tiles - 1, lines, width), F32),
            pltpu.VMEM((lines, width), F32),
            dma(3),
            dma(2, len(OFFSETS)),
            dma(2, len(OFFSETS)),
            dma(2, chunks),
            dma(2, chunks * others),
            dma(chunks, tiles - 1),
            dma(tiles - 1),
            dma(2, members - 1),
            dma(2, members - 1),
            dma(2, tiles - 1),
            dma(2, tiles - 1),
            dma(2),
        ],
        compiler_params=remote_params(0),
        name="whole",
    )(links, state, kern, *vectors, cot, w_in, w_out)


def finish_kernel(
    taps, factor, big_ref, small_ref, new_ref, sgrad_ref,
    new_out, sgrad_out, win_ref, wout_ref, kern_ref, bin_ref, ch_ref, sems,
):
    members, _, rows, width = big_ref.shape
    lines = small_ref.shape[1]
    copies = [
        pltpu.make_async_copy(source, target, sems.at[k])
        for k, (source, target) in enumerate([(new_ref, new_out), (sgrad_ref, sgrad_out)])
    ]
    for copy in copies:
        copy.start()
    for m in range(members):
        win_ref[pl.ds(m * rows, rows), :] = big_ref[m, 0].astype(F32) * factor
        wout_ref[pl.ds(m * rows, rows), :] = big_ref[m, 1].astype(F32) * factor

    def line(at):
        return small_ref[at // lines, pl.ds(at % lines, 1), :] * factor

    for at in range(taps * taps):
        kern_ref[at // taps, pl.ds(at % taps, 1), :] = line(at)
    first = taps * taps
    extra = bin_ref.shape[0] // width
    for at in range(extra):
        bin_ref[pl.ds(at * width, width)] = line(first + at).reshape(width)
    for at in range(5):
        ch_ref[pl.ds(at, 1), :] = line(first + extra + at)
    for copy in copies:
        copy.wait()


def finish(big, small, new, sgrad, share, taps, hidden, factor):
    width = big.shape[3]
    shapes = [(share, width), (share, width), (taps, taps, width), (hidden,), (5, width)]
    anywhere = pl.BlockSpec(memory_space=pl.ANY)
    return pl.pallas_call(
        functools.partial(finish_kernel, taps, factor),
        in_specs=[vmem_spec()] * 2 + [anywhere] * 2,
        out_specs=[anywhere] * 2 + [vmem_spec()] * 5,
        out_shape=[jax.ShapeDtypeStruct(new.shape, BF16)] * 2
        + [jax.ShapeDtypeStruct(shape, F32) for shape in shapes],
        scratch_shapes=[pltpu.SemaphoreType.DMA((2,))],
        compiler_params=local_params(),
        name="finish",
    )(big, small, new, sgrad)


def body(
    state,
    cotangent,
    neighbors,
    kernel,
    conv_bias,
    norm_gain,
    norm_shift,
    w_in,
    bias_in,
    w_out,
    bias_out,
    layer_scale,
):
    side, width = state.shape[2], state.shape[4]
    cells = side * side
    center = state.reshape(cells, width)
    cot = cotangent.reshape(cells, width)
    hidden = w_in.shape[1]
    taps = kernel.shape[0]
    tiles = lax.axis_size("tile")
    members = lax.axis_size("member")
    vectors = (conv_bias, norm_gain, norm_shift, bias_in, bias_out, layer_scale)
    new_tile, state_grad, big, small = run_whole(
        neighbors, center, cot, kernel, vectors, w_in, w_out, side, members, tiles
    )
    share = hidden // tiles
    factor = 1.0 / math.sqrt(members * tiles * cells)
    new_tile, state_grad, win_share, *shares = finish(
        big, small, new_tile, state_grad, share, taps, hidden, factor
    )
    return (
        new_tile.reshape(state.shape),
        state_grad.reshape(state.shape),
        win_share.T,
        *shares,
    )


def solution(mesh):
    tiled = P("member", "tile", None, None, None)
    in_specs = (tiled, tiled) + (P(),) * 10
    out_specs = (tiled, tiled, P(None, "tile"), P("tile", None), P(), P(), P())
    return jax.shard_map(body, mesh=mesh, in_specs=in_specs, out_specs=out_specs, check_vma=False)
```

```python
import functools
import math

import jax
import jax.numpy as jnp
from jax import lax
from jax.experimental import pallas as pl
from jax.experimental.pallas import tpu as pltpu
from jax.sharding import PartitionSpec as P

OFFSETS = (1, 2, 3, -1, -2, -3)
GELU_SCALE = 0.7978845608028654
GELU_CUBIC = 0.044715
EPSILON = 1e-06
LANES = 128
LEAD = 8
MESH = pl.DeviceIdType.MESH
F32 = jnp.float32
BF16 = jnp.bfloat16
VMEM_LIMIT = 56 << 20


def vmem_spec():
    return pl.BlockSpec(memory_space=pltpu.VMEM)


def smem_spec():
    return pl.BlockSpec(memory_space=pltpu.SMEM)


def local_params():
    return pltpu.CompilerParams(vmem_limit_bytes=VMEM_LIMIT)


def remote_params(ident):
    return pltpu.CompilerParams(
        collective_id=ident, has_side_effects=True, vmem_limit_bytes=VMEM_LIMIT
    )


def pitch_of(side):
    return side + 2 * LEAD


def spread_of(side, margin):
    return (side + 2 * margin) * pitch_of(side)


def place(padded, side, margin, center):
    pitch = pitch_of(side)
    for part in range(padded.shape[0]):

        def clear(row, carry):
            at = pl.ds(pl.multiple_of(row * pitch, 8), pitch)
            padded[part, at, :] = jnp.zeros((pitch, LANES), F32)
            return carry

        lax.fori_loop(0, side + 2 * margin, clear, 0)

        def put(row, carry):
            at = pl.ds(pl.multiple_of((margin + row) * pitch + LEAD, 8), side)
            padded[part, at, :] = center(part, row)
            return carry

        lax.fori_loop(0, side, put, 0)


def around(tile, count):
    takers = [lax.rem(tile + offset + count, count) for offset in OFFSETS]
    givers = [lax.rem(tile - offset + count, count) for offset in OFFSETS]
    return takers, givers


def pack(padded, side, margin, want, send_ref):
    pitch = pitch_of(side)
    edge = side - margin
    for part in range(padded.shape[0]):
        lanes = pl.ds(part * LANES, LANES)
        for k in range(margin):
            low = (margin + k) * pitch + LEAD
            high = (margin + edge + k) * pitch + LEAD
            first = margin * pitch + LEAD
            lines = [
                padded[part, pl.ds(low, side), :],
                padded[part, pl.ds(high, side), :],
                padded[part, pl.ds(first + k, side, stride=pitch), :],
                padded[part, pl.ds(first + edge + k, side, stride=pitch), :],
            ]
            lines = lines + [
                jnp.concatenate([lines[0][:8]] * (side // 8), axis=0),
                jnp.concatenate([lines[0][side - 8 :]] * (side // 8), axis=0),
                jnp.concatenate([lines[1][:8]] * (side // 8), axis=0),
                jnp.concatenate([lines[1][side - 8 :]] * (side // 8), axis=0),
            ]
            for slot in range(len(OFFSETS)):
                line = lines[7]
                for way in range(7):
                    line = jnp.where(want[slot][way], lines[way], line)
                send_ref[slot, k, :, lanes] = line.astype(BF16)


def unpack(padded, side, margin, have, recv_ref, flank):
    pitch = pitch_of(side)
    for part in range(padded.shape[0]):
        lanes = pl.ds(part * LANES, LANES)
        for k in range(margin):
            lines = [recv_ref[slot, k, :, lanes].astype(F32) for slot in range(len(OFFSETS))]
            for way in range(8):
                size = side if way < 4 else 8
                line = jnp.zeros((size, LANES), F32)
                for slot in range(len(OFFSETS)):
                    line = jnp.where(have[slot][way], lines[slot][:size], line)
                if way == 0:
                    at = pl.ds((margin + side + k) * pitch + LEAD, side)
                elif way == 1:
                    at = pl.ds(k * pitch + LEAD, side)
                elif way == 2:
                    at = pl.ds(margin * pitch + LEAD + side + k, side, stride=pitch)
                elif way == 3:
                    at = pl.ds(margin * pitch + LEAD - margin + k, side, stride=pitch)
                else:
                    row = margin + side + k if way in (4, 5) else k
                    at = pl.ds(row * pitch + (LEAD + side if way in (4, 6) else LEAD - 8), 8)
                padded[part, at, :] = line
                if way in (2, 3):
                    far = 3 - way
                    blank = jnp.zeros((LEAD, LANES), F32)
                    flank[far, k, part, pl.ds(0, LEAD), :] = blank
                    flank[far, k, part, pl.ds(LEAD, side), :] = line
                    flank[far, k, part, pl.ds(LEAD + side, LEAD), :] = blank


def prepare(source, target, sems, slot, **device):
    return pltpu.make_async_remote_copy(
        src_ref=source,
        dst_ref=target,
        send_sem=sems.at[0, slot],
        recv_sem=sems.at[1, slot],
        device_id=device,
        device_id_type=MESH,
    )


def remote(source, target, sems, slot, **device):
    copy = prepare(source, target, sems, slot, **device)
    copy.start()
    return copy


def strip_to(slot, send_ref, recv_ref, sems, count):
    tile = lax.axis_index("tile")
    takers, _ = around(tile, count)
    return prepare(send_ref.at[slot], recv_ref.at[slot], sems, slot, tile=takers[slot])


def idle(slot, count, receiving):
    tile = lax.axis_index("tile")
    if abs(OFFSETS[slot]) < 3:
        return None
    low = (OFFSETS[slot] > 0) == receiving
    ends = (0, 2) if low else (count - 3, count - 1)
    return jnp.logical_or(tile == ends[0], tile == ends[1])


def unless(condition, act):
    if condition is None:
        act()
    else:
        pl.when(jnp.logical_not(condition))(act)


def swap_halo(padded, side, margin, links_ref, send_ref, recv_ref, sems, count, ready):
    tile = lax.axis_index("tile")
    takers, _ = around(tile, count)
    want = [[links_ref[taker, way] == tile for way in range(8)] for taker in takers]
    pack(padded, side, margin, want, send_ref)
    ready()
    for slot in range(len(OFFSETS)):
        unless(
            idle(slot, count, False),
            lambda slot=slot: strip_to(slot, send_ref, recv_ref, sems, count).start(),
        )


def wait_halo(send_ref, recv_ref, sems, count):
    for slot in range(len(OFFSETS)):
        copy = strip_to(slot, send_ref, recv_ref, sems, count)
        unless(idle(slot, count, False), copy.wait_send)
        unless(idle(slot, count, True), copy.wait_recv)


def take_halo(padded, side, margin, links_ref, recv_ref, count, flank):
    tile = lax.axis_index("tile")
    _, givers = around(tile, count)
    have = [[links_ref[tile, way] == giver for way in range(8)] for giver in givers]
    unpack(padded, side, margin, have, recv_ref, flank)


def packed_of(side, margin):
    return (side // 2 + 2 * margin) * (side // 8 + 2 * margin)


def regroup(padded, packed, side, margin):
    pitch = pitch_of(side)
    step = side // 8
    columns = step + 2 * margin

    def row(up, carry):
        for col in range(columns):
            values = [
                padded[
                    part,
                    pl.ds((side // 2 * half + up) * pitch + LEAD - margin + col, 8, stride=step),
                    :,
                ]
                for half in range(2)
                for part in range(padded.shape[0])
            ]
            packed[up * columns + col] = jnp.concatenate(values, axis=1).astype(BF16)
        return carry

    lax.fori_loop(0, side // 2 + 2 * margin, row, 0)


def spread_taps(kern_ref, taps_ref, taps):
    for a in range(taps):
        for b in range(taps):
            line = kern_ref[a, pl.ds(b, 1), :]
            line = jnp.concatenate([line, line], axis=1)
            taps_ref[a * taps + b] = jnp.broadcast_to(line, taps_ref.shape[1:]).astype(BF16)


def convolve_wide(padded, part, kern_ref, side, taps, emit, group=4):
    pitch = pitch_of(side)
    margin = taps // 2
    lanes = pl.ds(part * LANES, LANES)

    def step(index, carry):
        base = index * group
        total = [jnp.zeros((side, LANES), F32) for _ in range(group)]
        for col in range(taps):
            for row in range(group + taps - 1):
                start = (base + row) * pitch
                line = padded[part, pl.ds(start + (LEAD - margin + col), side), :]
                for out in range(group):
                    up = row - out
                    if 0 <= up < taps:
                        total[out] = total[out] + kern_ref[up, pl.ds(col, 1), lanes] * line
        for out in range(group):
            emit(pl.multiple_of((base + out) * side, side), total[out])
        return carry

    lax.fori_loop(0, side // group, step, 0)


def convolve(packed, taps_ref, side, taps, emit, begin, end, group=8):
    step = side // 8
    columns = step + taps - 1
    parts = packed.shape[2] // (2 * LANES)
    for pair in range(begin, end):
        lanes = pl.ds(pair * 2 * LANES, 2 * LANES)

        def block(index, carry):
            base = lax.div(index, step) * group
            col = lax.rem(index, step)
            total = [jnp.zeros((8, 2 * LANES), F32) for _ in range(group)]
            for b in range(taps):
                lines = [
                    packed[(base + row) * columns + col + b, :, lanes]
                    for row in range(group + taps - 1)
                ]
                sums = [None] * group
                for a in range(taps):
                    spot = (taps - 1 - a) * taps + taps - 1 - b
                    weight = taps_ref[spot, :, lanes]
                    for out in range(group):
                        product = weight * lines[out + a]
                        sums[out] = product if a == 0 else sums[out] + product
                for out in range(group):
                    total[out] = total[out] + sums[out].astype(F32)
            for out in range(group):
                for lane in range(2):
                    place = 2 * pair + lane
                    row = side // 2 * (place // parts) + base + out
                    at = pl.ds(row * side + col, 8, stride=step)
                    emit(place % parts, at, total[out][:, lane * LANES : (lane + 1) * LANES])
            return carry

        lax.fori_loop(0, step * (side // 2 // group), block, 0)


def kernel_grad(packed, gpacked, target, pair, side, taps, group=8):
    margin = taps // 2
    step = side // 8
    columns = step + taps - 1
    lanes = pl.ds(pair * 2 * LANES, 2 * LANES)

    def over(b, carry):
        sums = [jnp.zeros((8, 2 * LANES), F32) for _ in range(taps)]
        for col in range(step):
            for base in range(0, side // 2, group):
                grads = [
                    gpacked[(base + row + margin) * columns + col + margin, :, lanes]
                    for row in range(group)
                ]
                lines = [
                    packed[(base + row) * columns + col + b, :, lanes]
                    for row in range(group + taps - 1)
                ]
                for a in range(taps):
                    products = [grads[row] * lines[row + a] for row in range(group)]
                    while len(products) > 1:
                        products = [x + y for x, y in zip(products[::2], products[1::2])]
                    sums[a] = sums[a] + products[0].astype(F32)
        for a in range(taps):
            target[b, pl.ds(a, 1), lanes] = jnp.sum(sums[a], axis=0, keepdims=True)
        return carry

    lax.fori_loop(0, taps, over, 0)


ORDER = (0, 3, 1, 2)


def correct(padded, flank, part, kern_ref, side, taps, flipped, target):
    pitch = pitch_of(side)
    margin = taps // 2
    lanes = pl.ds(part * LANES, LANES)

    def weight(a, b):
        if flipped:
            a, b = taps - 1 - a, taps - 1 - b
        return kern_ref[a, pl.ds(b, 1), lanes]

    for far in range(2):
        for out in range(margin):
            row = side - margin + out if far else out
            total = jnp.zeros((side, LANES), F32)
            for near in range(margin):
                up = margin + side + near - row if far else near - row
                if 0 <= up < taps:
                    start = (margin + side + near if far else near) * pitch + LEAD - margin
                    for col in range(taps):
                        total = total + weight(up, col) * padded[part, pl.ds(start + col, side), :]
            target[part, pl.ds(row * side, side), :] += total
        for out in range(margin):
            col = side - margin + out if far else out
            total = jnp.zeros((side, LANES), F32)
            for near in range(margin):
                over = margin + side + near - col if far else near - col
                if 0 <= over < taps:
                    for row in range(taps):
                        line = flank[far, near, part, pl.ds(LEAD - margin + row, side), :]
                        total = total + weight(row, over) * line
            at = pl.ds(col, side, stride=side)
            target[part, at, :] = target[part, at, :] + total


def contract_rows(left, right):
    return lax.dot_general(left, right, (((0,), (0,)), ((), ())), preferred_element_type=F32)


def contract_cols(left, right):
    return lax.dot_general(left, right, (((1,), (1,)), ((), ())), preferred_element_type=F32)


def whole_kernel(
    side,
    taps,
    members,
    tiles,
    chunk,
    block,
    links_ref,
    state_ref,
    kern_ref,
    cbias_ref,
    gain_ref,
    shift_ref,
    bin_ref,
    bout_ref,
    scale_ref,
    cot_hbm,
    win_hbm,
    wout_hbm,
    new_hbm,
    sgrad_hbm,
    out_ref,
    sout_ref,
    padded,
    gpad,
    flank,
    packed,
    gpacked,
    taps_ref,
    gkern_ref,
    mixed_ref,
    inv_ref,
    normed_ref,
    low_ref,
    act_ref,
    glow_ref,
    branch_ref,
    gnorm_ref,
    gmix_ref,
    gbin_ref,
    gch_ref,
    cot_ref,
    win_ref,
    wout_ref,
    new_ref,
    sgrad_ref,
    send,
    recv,
    gsend,
    grecv,
    big,
    core_in,
    a_x,
    b_x,
    c_x,
    d_x,
    a_y,
    b_y,
    c_y,
    d_y,
    e_out,
    f_in,
    own,
    s_pack,
    s_send,
    sm_in,
    st_out,
    st_in,
    s_own,
    load_sem,
    halo_sem,
    ghalo_sem,
    core_sem,
    bx_sem,
    dx_sem,
    by_sem,
    dy_sem,
    f_send,
    f_recv,
    g_sem,
    sm_sem,
    st_sem,
    sg_sem,
    store_sem,
):
    margin = taps // 2
    parts = padded.shape[0]
    cells = side * side
    groups = side // 4
    pitch = pitch_of(side)
    hidden = win_ref.shape[1]
    width = win_ref.shape[0]
    fourth = hidden // 4
    chunks = 2
    per = tiles // chunks
    spots = members // 2
    rows = hidden // (tiles * members)
    member = lax.axis_index("member")
    tile = lax.axis_index("tile")
    core = lax.rem(member, 2)
    cross = member // 2
    odd = lax.rem(tile, 2)
    quarter = tiles // 4
    half_per = per // 2
    along = [lax.rem(tile + 2 * k, tiles) for k in range(1, tiles // 2)]
    mates = [lax.rem(member + k, members) for k in range(1, members)]
    peers = [lax.rem(tile + k, tiles) for k in range(1, tiles)]
    barrier = pltpu.get_barrier_semaphore()
    for mate in mates:
        pl.semaphore_signal(barrier, inc=1, device_id={"member": mate}, device_id_type=MESH)
    for peer in peers:
        pl.semaphore_signal(barrier, inc=1, device_id={"tile": peer}, device_id_type=MESH)
    moves = [(cot_hbm, cot_ref)]
    for k, source in enumerate(ORDER):
        old, new = pl.ds(source * fourth, fourth), pl.ds(k * fourth, fourth)
        moves.append((win_hbm.at[:, old], win_ref.at[:, new]))
        moves.append((wout_hbm.at[old, :], wout_ref.at[new, :]))
    loads = [
        pltpu.make_async_copy(source, target, load_sem.at[k])
        for k, (source, target) in enumerate(moves)
    ]
    for load in loads:
        load.start()

    def center(part, row):
        at = pl.ds(pl.multiple_of(row * side, side), side)
        return state_ref[at, pl.ds(part * LANES, LANES)].astype(F32)

    place(padded, side, margin, center)
    swap_halo(
        padded, side, margin, links_ref, send, recv, halo_sem, tiles,
        lambda: pl.semaphore_wait(barrier, members + tiles - 2),
    )

    def forward_emit(part):
        bias = cbias_ref[pl.ds(part * LANES, LANES)].reshape(1, LANES)

        def emit(start, value):
            mixed_ref[part, pl.ds(start, side), :] = value + bias

        return emit

    for part in range(parts):
        convolve_wide(padded, part, kern_ref, side, taps, forward_emit(part))
    spread_taps(kern_ref, taps_ref, taps)
    wait_halo(send, recv, halo_sem, tiles)
    take_halo(padded, side, margin, links_ref, recv, tiles, flank)
    for part in range(parts):
        correct(padded, flank, part, kern_ref, side, taps, False, mixed_ref)

    gbin_ref[...] = jnp.zeros_like(gbin_ref)
    gch_ref[...] = jnp.zeros_like(gch_ref)
    for load in loads:
        load.wait()

    def prepare_cells(at):
        mixed = jnp.concatenate([mixed_ref[part, at, :] for part in range(parts)], axis=1)
        centered = mixed - jnp.mean(mixed, axis=1, keepdims=True)
        variance = jnp.mean(centered * centered, axis=1, keepdims=True)
        inv_std = lax.rsqrt(variance + EPSILON)
        norm_hat = centered * inv_std
        for part in range(parts):
            mixed_ref[part, at, :] = norm_hat[:, part * LANES : (part + 1) * LANES]
        inv_ref[at, :] = jnp.broadcast_to(inv_std, (block, LANES))
        normed_ref[at, :] = (norm_hat * gain_ref[...].reshape(1, -1) + shift_ref[...].reshape(1, -1)).astype(BF16)
        grad_branch = scale_ref[...].reshape(1, -1) * cot_ref[at, :].astype(F32)
        low_ref[at, :] = grad_branch.astype(BF16)
        gch_ref[3:4, :] += jnp.sum(grad_branch, axis=0, keepdims=True)

    def finish_cells(at, branch, grad_normed):
        gain = gain_ref[...].reshape(1, -1)
        branch = branch + bout_ref[...].reshape(1, -1)
        scaled_branch = scale_ref[...].reshape(1, -1) * branch
        new_ref[at, :] = (state_ref[at, :].astype(F32) + scaled_branch).astype(BF16)
        norm_hat = jnp.concatenate([mixed_ref[part, at, :] for part in range(parts)], axis=1)
        scaled = grad_normed * gain
        inner = (
            scaled
            - jnp.mean(scaled, axis=1, keepdims=True)
            - norm_hat * jnp.mean(scaled * norm_hat, axis=1, keepdims=True)
        )
        inv_std = inv_ref[at, :]
        for part in range(parts):
            lanes = slice(part * LANES, (part + 1) * LANES)
            grad_mixed = inv_std * inner[:, lanes]
            gmix_ref[part, at, :] = grad_mixed
            gch_ref[0:1, lanes] += jnp.sum(grad_mixed, axis=0, keepdims=True)
        gch_ref[1:2, :] += jnp.sum(grad_normed * norm_hat, axis=0, keepdims=True)
        gch_ref[2:3, :] += jnp.sum(grad_normed, axis=0, keepdims=True)
        gch_ref[4:5, :] += jnp.sum(cot_ref[at, :].astype(F32) * branch, axis=0, keepdims=True)

    def exchange_core(h):
        return [
            prepare(
                big.at[h, :, :, :, :, 1 - core], core_in.at[h], core_sem, h,
                member=cross * 2 + 1 - core,
            )
        ]

    def across(source, target, sems, h):
        copies = []
        for k in range(1, spots):
            spot = lax.rem(cross + k, spots)
            copies.append(
                prepare(
                    source.at[h, spot], target.at[h, k - 1], sems, h * (spots - 1) + k - 1,
                    member=spot * 2 + core,
                )
            )
        return copies

    def sideways(source, target, sems, h):
        return [prepare(source.at[h, 1 - odd], target.at[h], sems, h, tile=tile + 1 - 2 * odd)]

    def first_hop(h):
        return across(a_x, b_x, bx_sem, h) + sideways(a_y, b_y, by_sem, h)

    def second_hop(h):
        return sideways(c_y, d_y, dy_sem, h) + across(c_x, d_x, dx_sem, h)

    def spot_of(other):
        place = lax.div(other, 2)
        half = quarter // 2
        outer = jnp.logical_or(place < half, place >= 3 * half)
        at = jnp.where(place < half, place, jnp.where(outer, place - 2 * half, place - half))
        return outer, at

    def third_hop(h, k):
        other = along[k]
        outer, at = spot_of(other)
        return pltpu.make_async_remote_copy(
            src_ref=e_out.at[h, jnp.clip(at, 0, half_per - 1)],
            dst_ref=f_in.at[k],
            send_sem=f_send.at[h, k],
            recv_sem=f_recv.at[k],
            device_id={"tile": other},
            device_id_type=MESH,
        )

    def goes(h, k):
        outer, at = spot_of(along[k])
        return outer if h == 0 else jnp.logical_not(outer)

    def start_first(h):
        for copy in exchange_core(h):
            copy.wait()

        def add(j, carry):
            for y in range(2):
                for x in range(spots):
                    for kind in range(2):
                        value = big[h, kind, j, y, x, core].astype(F32) + core_in[h, kind, j, y, x].astype(F32)
                        if kind == 0:
                            a_x[h, x, j, y] = value.astype(BF16)
                        else:
                            a_y[h, y, j, x] = value.astype(BF16)
            return carry

        lax.fori_loop(0, half_per, add, 0)
        for copy in first_hop(h):
            copy.start()

    def start_second(h):
        for copy in first_hop(h):
            copy.wait()

        def add(j, carry):
            for y in range(2):
                value = a_x[h, cross, j, y].astype(F32)
                for k in range(spots - 1):
                    value = value + b_x[h, k, j, y].astype(F32)
                c_y[h, y, j] = value.astype(BF16)
            for x in range(spots):
                value = a_y[h, odd, j, x].astype(F32) + b_y[h, j, x].astype(F32)
                c_x[h, x, j] = value.astype(BF16)
            return carry

        lax.fori_loop(0, half_per, add, 0)
        for copy in second_hop(h):
            copy.start()

    def start_third(h):
        for copy in second_hop(h):
            copy.wait()

        def add(j, carry):
            value = c_y[h, odd, j].astype(F32) + d_y[h, j].astype(F32)
            e_out[h, j, 0] = value.astype(BF16)
            value = c_x[h, cross, j].astype(F32)
            for k in range(spots - 1):
                value = value + d_x[h, k, j].astype(F32)
            e_out[h, j, 1] = value.astype(BF16)
            return carry

        lax.fori_loop(0, half_per, add, 0)
        for k in range(len(along)):

            @pl.when(goes(h, k))
            def _():
                third_hop(h, k).start()

    def bias_of(h):
        quarters = [bin_ref[pl.ds(k * fourth, fourth)].reshape(1, fourth) for k in ORDER[2 * h : 2 * h + 2]]
        return jnp.concatenate(quarters, axis=1)

    def mlp(h, r):
        at = pl.ds(pl.multiple_of(r * block, block), block)
        if h == 0:
            prepare_cells(at)
        here = slice(h * chunk, (h + 1) * chunk)
        win = win_ref[:, here]
        wout = wout_ref[here, :]
        pre = jnp.dot(normed_ref[at, :], win, preferred_element_type=F32) + bias_of(h)
        square = pre * pre
        tanh_value = jnp.tanh(GELU_SCALE * pre * (1.0 + GELU_CUBIC * square))
        half = 0.5 * (1.0 + tanh_value)
        activation = (pre * half).astype(BF16)
        slope = half + (0.5 * GELU_SCALE) * pre * (1.0 - tanh_value * tanh_value) * (
            1.0 + 3.0 * GELU_CUBIC * square
        )
        grad_pre = contract_cols(low_ref[at, :], wout) * slope
        grad_low = grad_pre.astype(BF16)
        act_ref[at, :] = activation
        glow_ref[at, :] = grad_low
        gbin_ref[:, here] += jnp.sum(grad_pre, axis=0, keepdims=True)
        if h == 0:
            branch_ref[at, :] = jnp.dot(activation, wout, preferred_element_type=F32)
            gnorm_ref[at, :] = contract_cols(grad_low, win)

    def close_cells(h, r):
        at = pl.ds(pl.multiple_of(r * block, block), block)
        here = slice(h * chunk, (h + 1) * chunk)
        branch = jnp.dot(act_ref[at, :], wout_ref[here, :], preferred_element_type=F32)
        grad_normed = contract_cols(glow_ref[at, :], win_ref[:, here])
        finish_cells(at, branch_ref[at, :] + branch, gnorm_ref[at, :] + grad_normed)

    def weights(h):
        for kind, (left, right) in enumerate([(glow_ref, normed_ref), (act_ref, low_ref)]):
            value = contract_rows(left[...], right[...])
            for index in range(per * members):
                j, y = index // members // 2, index // members % 2
                x, c = index % members // 2, index % 2
                big[h, kind, j, y, x, c] = value[index * rows : (index + 1) * rows].astype(BF16)
        for copy in exchange_core(h):
            copy.start()

    def inner_step(r, carry):
        mlp(0, r)
        return carry

    def outer_step(r, carry):
        mlp(1, r)

        @pl.when(r == 0)
        def _():
            start_first(0)

        return carry

    def close_step(r, carry):
        close_cells(1, r)

        @pl.when(r == 0)
        def _():
            start_first(1)

        return carry

    lax.fori_loop(0, cells // block, inner_step, 0)
    weights(0)
    lax.fori_loop(0, cells // block, outer_step, 0)
    weights(1)
    lax.fori_loop(0, cells // block, close_step, 0)
    start_second(0)
    new_copy = pltpu.make_async_copy(new_ref, new_hbm, store_sem.at[0])
    new_copy.start()

    def gcenter(part, row):
        at = pl.ds(pl.multiple_of(row * side, side), side)
        return gmix_ref[part, at, :].astype(BF16).astype(F32)

    place(gpad, side, margin, gcenter)
    swap_halo(
        gpad, side, margin, links_ref, gsend, grecv, ghalo_sem, tiles, lambda: None
    )
    lines = s_pack.shape[1]
    s_pack[...] = jnp.zeros_like(s_pack)
    first = taps * taps
    extra = gbin_ref.shape[1] // width
    for row in range(extra):
        at = first + row
        s_pack[at // lines, pl.ds(at % lines, 1), :] = gbin_ref[:, pl.ds(ORDER.index(row) * width, width)]
    for row in range(5):
        at = first + extra + row
        s_pack[at // lines, pl.ds(at % lines, 1), :] = gch_ref[pl.ds(row, 1), :]

    def emit(part, at, value):
        mixed_ref[part, at, :] = value

    regroup(padded, packed, side, margin)
    regroup(gpad, gpacked, side, margin)
    kernel_grad(packed, gpacked, gkern_ref, 0, side, taps)
    start_third(0)
    kernel_grad(packed, gpacked, gkern_ref, 1, side, taps)
    start_second(1)
    kernel_grad(packed, gpacked, gkern_ref, 2, side, taps)
    for up in range(taps):
        for col in range(taps):
            at = up * taps + col
            line = gkern_ref[col, up : up + 1, :]
            s_pack[at // lines, pl.ds(at % lines, 1), :] = line[:, :width] + line[:, width:]
    flat = s_pack.reshape(s_send.shape)
    s_send[...] = flat[...].astype(BF16)
    small = [remote(s_send, sm_in.at[k], sm_sem, k, member=mate) for k, mate in enumerate(mates)]
    convolve(gpacked, taps_ref, side, taps, emit, 0, 2)
    start_third(1)
    for copy in small:
        copy.wait()
    for row in range(tiles):
        at = pl.ds(row * lines, lines)
        total = s_pack[row]
        for k in range(members - 1):
            total = total + sm_in[k, at, :].astype(F32)
        st_out[row] = total
    small = [
        remote(st_out.at[peer], st_in.at[k], st_sem, k, tile=peer) for k, peer in enumerate(peers)
    ]
    convolve(gpacked, taps_ref, side, taps, emit, 2, 3)
    wait_halo(gsend, grecv, ghalo_sem, tiles)
    take_halo(gpad, side, margin, links_ref, grecv, tiles, flank)
    for part in range(parts):
        lanes = pl.ds(part * LANES, LANES)
        correct(gpad, flank, part, kern_ref, side, taps, True, mixed_ref)

        def close(row, carry):
            at = pl.ds(pl.multiple_of(row * LANES, LANES), LANES)
            sgrad_ref[at, lanes] = (cot_ref[at, lanes].astype(F32) + mixed_ref[part, at, :]).astype(BF16)
            return carry

        lax.fori_loop(0, cells // LANES, close, 0)
    store = pltpu.make_async_copy(sgrad_ref, sgrad_hbm, store_sem.at[1])
    store.start()
    for copy in small:
        copy.wait()
    total = st_out[tile]
    for k in range(tiles - 1):
        total = total + st_in[k]
    s_own[...] = total
    sout_ref[tile] = total
    small = [
        remote(s_own, sout_ref.at[tile], sg_sem, k, tile=peer) for k, peer in enumerate(peers)
    ]
    for k in range(len(along)):
        third_hop(0, k).wait_recv()
        for h in range(chunks):

            @pl.when(goes(h, k))
            def _():
                third_hop(h, k).wait_send()

    outer, at = spot_of(tile)
    for h in range(chunks):

        @pl.when(outer if h == 0 else jnp.logical_not(outer))
        def _():
            for kind in range(2):
                value = e_out[h, jnp.clip(at, 0, half_per - 1), kind].astype(F32)
                for k in range(len(along)):
                    value = value + f_in[k, kind].astype(F32)
                own[kind] = value.astype(BF16)

    out_ref[member] = own[...]
    back = [
        remote(own, out_ref.at[member], g_sem, k, member=mate) for k, mate in enumerate(mates)
    ]
    for copy in small + back:
        copy.wait()
    new_copy.wait()
    store.wait()


def run_whole(links, state, cot, kern, vectors, w_in, w_out, side, members, tiles, chunk=768, block=512):
    cells, width = state.shape
    hidden = w_in.shape[1]
    taps = kern.shape[0]
    margin = taps // 2
    chunks = 2
    half = tiles // chunks // 2
    spots = members // 2
    rows = hidden // (tiles * members)
    piece = lambda *n: pltpu.VMEM((chunks, *n, rows, width), BF16)
    used = taps * taps + hidden // width + 5
    lines = 8 * (-(-used // (8 * tiles)))
    others = max(spots - 1, 1)
    parts = width // LANES
    spread = spread_of(side, margin)
    dma = lambda *n: pltpu.SemaphoreType.DMA(n)
    strips = (len(OFFSETS), margin, side, width)
    anywhere = pl.BlockSpec(memory_space=pl.ANY)
    return pl.pallas_call(
        functools.partial(whole_kernel, side, taps, members, tiles, chunk, block),
        in_specs=[smem_spec()] + [vmem_spec()] * 8 + [anywhere] * 3,
        out_specs=[anywhere] * 2 + [vmem_spec()] * 2,
        out_shape=[
            jax.ShapeDtypeStruct((cells, width), BF16),
            jax.ShapeDtypeStruct((cells, width), BF16),
            jax.ShapeDtypeStruct((members, 2, rows, width), BF16),
            jax.ShapeDtypeStruct((tiles, lines, width), F32),
        ],
        scratch_shapes=[
            pltpu.VMEM((parts, spread, LANES), F32),
            pltpu.VMEM((parts, spread, LANES), F32),
            pltpu.VMEM((2, margin, parts, pitch_of(side), LANES), F32),
            pltpu.VMEM((packed_of(side, margin), 8, 2 * width), BF16),
            pltpu.VMEM((packed_of(side, margin), 8, 2 * width), BF16),
            pltpu.VMEM((taps * taps, 8, 2 * width), BF16),
            pltpu.VMEM((taps, 8, 2 * width), F32),
            pltpu.VMEM((parts, cells, LANES), F32),
            pltpu.VMEM((cells, LANES), F32),
            pltpu.VMEM((cells, width), BF16),
            pltpu.VMEM((cells, width), BF16),
            pltpu.VMEM((cells, chunk), BF16),
            pltpu.VMEM((cells, chunk), BF16),
            pltpu.VMEM((cells, width), F32),
            pltpu.VMEM((cells, width), F32),
            pltpu.VMEM((parts, cells, LANES), F32),
            pltpu.VMEM((1, hidden), F32),
            pltpu.VMEM((8, width), F32),
            pltpu.VMEM((cells, width), BF16),
            pltpu.VMEM((width, hidden), BF16),
            pltpu.VMEM((hidden, width), BF16),
            pltpu.VMEM((cells, width), BF16),
            pltpu.VMEM((cells, width), BF16),
            pltpu.VMEM(strips, BF16),
            pltpu.VMEM(strips, BF16),
            pltpu.VMEM(strips, BF16),
            pltpu.VMEM(strips, BF16),
            piece(2, half, 2, spots, 2),
            piece(2, half, 2, spots),
            piece(spots, half, 2),
            piece(others, half, 2),
            piece(spots, half),
            piece(others, half),
            piece(2, half, spots),
            piece(half, spots),
            piece(2, half),
            piece(half),
            piece(half, 2),
            pltpu.VMEM((tiles // 2 - 1, 2, rows, width), BF16),
            pltpu.VMEM((2, rows, width), BF16),
            pltpu.VMEM((tiles, lines, width), F32),
            pltpu.VMEM((tiles * lines, width), BF16),
            pltpu.VMEM((members - 1, tiles * lines, width), BF16),
            pltpu.VMEM((tiles, lines, width), F32),
            pltpu.VMEM((tiles - 1, lines, width), F32),
            pltpu.VMEM((lines, width), F32),
            dma(9),
            dma(2, len(OFFSETS)),
            dma(2, len(OFFSETS)),
            dma(2, chunks),
            dma(2, chunks * others),
            dma(2, chunks * others),
            dma(2, chunks),
            dma(2, chunks),
            dma(chunks, tiles // 2 - 1),
            dma(tiles // 2 - 1),
            dma(2, members - 1),
            dma(2, members - 1),
            dma(2, tiles - 1),
            dma(2, tiles - 1),
            dma(2),
        ],
        compiler_params=remote_params(0),
        name="whole",
    )(links, state, kern, *vectors, cot, w_in, w_out)


def finish_kernel(
    taps, factor, big_ref, small_ref, new_ref, sgrad_ref,
    new_out, sgrad_out, win_ref, wout_ref, kern_ref, bin_ref, ch_ref, held, sems,
):
    members, _, rows, width = big_ref.shape
    lines = small_ref.shape[1]
    pieces = held.shape[1]
    size = held.shape[2]
    inward, outward = [], []
    for k, (source, target) in enumerate([(new_ref, new_out), (sgrad_ref, sgrad_out)]):
        for piece in range(pieces):
            at = pl.ds(piece * size, size)
            here = held.at[k, piece]
            inward.append(pltpu.make_async_copy(source.at[at, :], here, sems.at[0, k, piece]))
            outward.append(pltpu.make_async_copy(here, target.at[at, :], sems.at[1, k, piece]))
    for copy in inward:
        copy.start()
    for m in range(members):
        win_ref[pl.ds(m * rows, rows), :] = big_ref[m, 0].astype(F32) * factor
        wout_ref[pl.ds(m * rows, rows), :] = big_ref[m, 1].astype(F32) * factor
    for come, go in zip(inward, outward):
        come.wait()
        go.start()

    def line(at):
        return small_ref[at // lines, pl.ds(at % lines, 1), :] * factor

    for at in range(taps * taps):
        kern_ref[at // taps, pl.ds(at % taps, 1), :] = line(at)
    first = taps * taps
    extra = bin_ref.shape[0] // width
    for at in range(extra):
        bin_ref[pl.ds(at * width, width)] = line(first + at).reshape(width)
    for at in range(5):
        ch_ref[pl.ds(at, 1), :] = line(first + extra + at)
    for copy in outward:
        copy.wait()


def finish(big, small, new, sgrad, share, taps, hidden, factor, pieces=4):
    width = big.shape[3]
    shapes = [(share, width), (share, width), (taps, taps, width), (hidden,), (5, width)]
    anywhere = pl.BlockSpec(memory_space=pl.ANY)
    return pl.pallas_call(
        functools.partial(finish_kernel, taps, factor),
        in_specs=[vmem_spec()] * 2 + [anywhere] * 2,
        out_specs=[anywhere] * 2 + [vmem_spec()] * 5,
        out_shape=[jax.ShapeDtypeStruct(new.shape, BF16)] * 2
        + [jax.ShapeDtypeStruct(shape, F32) for shape in shapes],
        scratch_shapes=[
            pltpu.VMEM((2, pieces, new.shape[0] // pieces, width), BF16),
            pltpu.SemaphoreType.DMA((2, 2, pieces)),
        ],
        compiler_params=local_params(),
        name="finish",
    )(big, small, new, sgrad)


def body(
    state,
    cotangent,
    neighbors,
    kernel,
    conv_bias,
    norm_gain,
    norm_shift,
    w_in,
    bias_in,
    w_out,
    bias_out,
    layer_scale,
):
    side, width = state.shape[2], state.shape[4]
    cells = side * side
    center = state.reshape(cells, width)
    cot = cotangent.reshape(cells, width)
    hidden = w_in.shape[1]
    taps = kernel.shape[0]
    tiles = lax.axis_size("tile")
    members = lax.axis_size("member")
    vectors = (conv_bias, norm_gain, norm_shift, bias_in, bias_out, layer_scale)
    new_tile, state_grad, big, small = run_whole(
        neighbors, center, cot, kernel, vectors, w_in, w_out, side, members, tiles
    )
    share = hidden // tiles
    factor = 1.0 / math.sqrt(members * tiles * cells)
    new_tile, state_grad, win_share, *shares = finish(
        big, small, new_tile, state_grad, share, taps, hidden, factor
    )
    return (
        new_tile.reshape(state.shape),
        state_grad.reshape(state.shape),
        win_share.T,
        *shares,
    )


def solution(mesh):
    tiled = P("member", "tile", None, None, None)
    in_specs = (tiled, tiled) + (P(),) * 10
    out_specs = (tiled, tiled, P(None, "tile"), P("tile", None), P(), P(), P())
    return jax.shard_map(body, mesh=mesh, in_specs=in_specs, out_specs=out_specs, check_vma=False)
```

```python
import functools
import math

import jax
import jax.numpy as jnp
from jax import lax
from jax.experimental import pallas as pl
from jax.experimental.pallas import tpu as pltpu
from jax.sharding import PartitionSpec as P

OFFSETS = (1, 2, 3, -1, -2, -3)
GELU_SCALE = 0.7978845608028654
GELU_CUBIC = 0.044715
EPSILON = 1e-06
LANES = 128
LEAD = 8
MESH = pl.DeviceIdType.MESH
F32 = jnp.float32
BF16 = jnp.bfloat16
VMEM_LIMIT = 56 << 20


def vmem_spec():
    return pl.BlockSpec(memory_space=pltpu.VMEM)


def smem_spec():
    return pl.BlockSpec(memory_space=pltpu.SMEM)


def local_params():
    return pltpu.CompilerParams(vmem_limit_bytes=VMEM_LIMIT)


def remote_params(ident):
    return pltpu.CompilerParams(
        collective_id=ident, has_side_effects=True, vmem_limit_bytes=VMEM_LIMIT
    )


def pitch_of(side):
    return side + 2 * LEAD


def spread_of(side, margin):
    return (side + 2 * margin) * pitch_of(side)


def place(padded, side, margin, center):
    pitch = pitch_of(side)
    for part in range(padded.shape[0]):

        def clear(row, carry):
            at = pl.ds(pl.multiple_of(row * pitch, 8), pitch)
            padded[part, at, :] = jnp.zeros((pitch, LANES), F32)
            return carry

        lax.fori_loop(0, side + 2 * margin, clear, 0)

        def put(row, carry):
            at = pl.ds(pl.multiple_of((margin + row) * pitch + LEAD, 8), side)
            padded[part, at, :] = center(part, row)
            return carry

        lax.fori_loop(0, side, put, 0)


def around(tile, count):
    takers = [lax.rem(tile + offset + count, count) for offset in OFFSETS]
    givers = [lax.rem(tile - offset + count, count) for offset in OFFSETS]
    return takers, givers


def pack(padded, side, margin, want, send_ref):
    pitch = pitch_of(side)
    edge = side - margin
    for part in range(padded.shape[0]):
        lanes = pl.ds(part * LANES, LANES)
        for k in range(margin):
            low = (margin + k) * pitch + LEAD
            high = (margin + edge + k) * pitch + LEAD
            first = margin * pitch + LEAD
            lines = [
                padded[part, pl.ds(low, side), :],
                padded[part, pl.ds(high, side), :],
                padded[part, pl.ds(first + k, side, stride=pitch), :],
                padded[part, pl.ds(first + edge + k, side, stride=pitch), :],
            ]
            lines = lines + [
                jnp.concatenate([lines[0][:8]] * (side // 8), axis=0),
                jnp.concatenate([lines[0][side - 8 :]] * (side // 8), axis=0),
                jnp.concatenate([lines[1][:8]] * (side // 8), axis=0),
                jnp.concatenate([lines[1][side - 8 :]] * (side // 8), axis=0),
            ]
            for slot in range(len(OFFSETS)):
                line = lines[7]
                for way in range(7):
                    line = jnp.where(want[slot][way], lines[way], line)
                send_ref[slot, k, :, lanes] = line.astype(BF16)


def unpack(padded, side, margin, have, recv_ref, flank):
    pitch = pitch_of(side)
    for part in range(padded.shape[0]):
        lanes = pl.ds(part * LANES, LANES)
        for k in range(margin):
            lines = [recv_ref[slot, k, :, lanes].astype(F32) for slot in range(len(OFFSETS))]
            for way in range(8):
                size = side if way < 4 else 8
                line = jnp.zeros((size, LANES), F32)
                for slot in range(len(OFFSETS)):
                    line = jnp.where(have[slot][way], lines[slot][:size], line)
                if way == 0:
                    at = pl.ds((margin + side + k) * pitch + LEAD, side)
                elif way == 1:
                    at = pl.ds(k * pitch + LEAD, side)
                elif way == 2:
                    at = pl.ds(margin * pitch + LEAD + side + k, side, stride=pitch)
                elif way == 3:
                    at = pl.ds(margin * pitch + LEAD - margin + k, side, stride=pitch)
                else:
                    row = margin + side + k if way in (4, 5) else k
                    at = pl.ds(row * pitch + (LEAD + side if way in (4, 6) else LEAD - 8), 8)
                padded[part, at, :] = line
                if way in (2, 3):
                    far = 3 - way
                    blank = jnp.zeros((LEAD, LANES), F32)
                    flank[far, k, part, pl.ds(0, LEAD), :] = blank
                    flank[far, k, part, pl.ds(LEAD, side), :] = line
                    flank[far, k, part, pl.ds(LEAD + side, LEAD), :] = blank


def prepare(source, target, sems, slot, **device):
    return pltpu.make_async_remote_copy(
        src_ref=source,
        dst_ref=target,
        send_sem=sems.at[0, slot],
        recv_sem=sems.at[1, slot],
        device_id=device,
        device_id_type=MESH,
    )


def remote(source, target, sems, slot, **device):
    copy = prepare(source, target, sems, slot, **device)
    copy.start()
    return copy


def strip_to(slot, send_ref, recv_ref, sems, count):
    tile = lax.axis_index("tile")
    takers, _ = around(tile, count)
    return prepare(send_ref.at[slot], recv_ref.at[slot], sems, slot, tile=takers[slot])


def idle(slot, count, receiving):
    tile = lax.axis_index("tile")
    if abs(OFFSETS[slot]) < 3:
        return None
    low = (OFFSETS[slot] > 0) == receiving
    ends = (0, 2) if low else (count - 3, count - 1)
    return jnp.logical_or(tile == ends[0], tile == ends[1])


def unless(condition, act):
    if condition is None:
        act()
    else:
        pl.when(jnp.logical_not(condition))(act)


def swap_halo(padded, side, margin, links_ref, send_ref, recv_ref, sems, count, ready):
    tile = lax.axis_index("tile")
    takers, _ = around(tile, count)
    want = [[links_ref[taker, way] == tile for way in range(8)] for taker in takers]
    pack(padded, side, margin, want, send_ref)
    ready()
    for slot in range(len(OFFSETS)):
        unless(
            idle(slot, count, False),
            lambda slot=slot: strip_to(slot, send_ref, recv_ref, sems, count).start(),
        )


def wait_halo(send_ref, recv_ref, sems, count):
    for slot in range(len(OFFSETS)):
        copy = strip_to(slot, send_ref, recv_ref, sems, count)
        unless(idle(slot, count, False), copy.wait_send)
        unless(idle(slot, count, True), copy.wait_recv)


def take_halo(padded, side, margin, links_ref, recv_ref, count, flank):
    tile = lax.axis_index("tile")
    _, givers = around(tile, count)
    have = [[links_ref[tile, way] == giver for way in range(8)] for giver in givers]
    unpack(padded, side, margin, have, recv_ref, flank)


def packed_of(side, margin):
    return (side // 2 + 2 * margin) * (side // 8 + 2 * margin)


def regroup(padded, packed, side, margin):
    pitch = pitch_of(side)
    step = side // 8
    columns = step + 2 * margin

    def row(up, carry):
        for col in range(columns):
            values = [
                padded[
                    part,
                    pl.ds((side // 2 * half + up) * pitch + LEAD - margin + col, 8, stride=step),
                    :,
                ]
                for half in range(2)
                for part in range(padded.shape[0])
            ]
            packed[up * columns + col] = jnp.concatenate(values, axis=1).astype(BF16)
        return carry

    lax.fori_loop(0, side // 2 + 2 * margin, row, 0)


def spread_taps(kern_ref, taps_ref, taps):
    for a in range(taps):
        for b in range(taps):
            line = kern_ref[a, pl.ds(b, 1), :]
            line = jnp.concatenate([line, line], axis=1)
            taps_ref[a * taps + b] = jnp.broadcast_to(line, taps_ref.shape[1:]).astype(BF16)


def convolve_wide(padded, part, kern_ref, side, taps, emit, group=4):
    pitch = pitch_of(side)
    margin = taps // 2
    lanes = pl.ds(part * LANES, LANES)

    def step(index, carry):
        base = index * group
        total = [jnp.zeros((side, LANES), F32) for _ in range(group)]
        for col in range(taps):
            for row in range(group + taps - 1):
                start = (base + row) * pitch
                line = padded[part, pl.ds(start + (LEAD - margin + col), side), :]
                for out in range(group):
                    up = row - out
                    if 0 <= up < taps:
                        total[out] = total[out] + kern_ref[up, pl.ds(col, 1), lanes] * line
        for out in range(group):
            emit(pl.multiple_of((base + out) * side, side), total[out])
        return carry

    lax.fori_loop(0, side // group, step, 0)


def convolve(packed, taps_ref, side, taps, emit, begin, end, group=8):
    step = side // 8
    columns = step + taps - 1
    parts = packed.shape[2] // (2 * LANES)
    for pair in range(begin, end):
        lanes = pl.ds(pair * 2 * LANES, 2 * LANES)

        def block(index, carry):
            base = lax.div(index, step) * group
            col = lax.rem(index, step)
            total = [jnp.zeros((8, 2 * LANES), F32) for _ in range(group)]
            for b in range(taps):
                lines = [
                    packed[(base + row) * columns + col + b, :, lanes]
                    for row in range(group + taps - 1)
                ]
                sums = [None] * group
                for a in range(taps):
                    spot = (taps - 1 - a) * taps + taps - 1 - b
                    weight = taps_ref[spot, :, lanes]
                    for out in range(group):
                        product = weight * lines[out + a]
                        sums[out] = product if a == 0 else sums[out] + product
                for out in range(group):
                    total[out] = total[out] + sums[out].astype(F32)
            for out in range(group):
                for lane in range(2):
                    place = 2 * pair + lane
                    row = side // 2 * (place // parts) + base + out
                    at = pl.ds(row * side + col, 8, stride=step)
                    emit(place % parts, at, total[out][:, lane * LANES : (lane + 1) * LANES])
            return carry

        lax.fori_loop(0, step * (side // 2 // group), block, 0)


def kernel_grad(packed, gpacked, target, pair, side, taps, group=8):
    margin = taps // 2
    step = side // 8
    columns = step + taps - 1
    lanes = pl.ds(pair * 2 * LANES, 2 * LANES)

    def over(b, carry):
        sums = [jnp.zeros((8, 2 * LANES), F32) for _ in range(taps)]
        for col in range(step):
            for base in range(0, side // 2, group):
                grads = [
                    gpacked[(base + row + margin) * columns + col + margin, :, lanes]
                    for row in range(group)
                ]
                lines = [
                    packed[(base + row) * columns + col + b, :, lanes]
                    for row in range(group + taps - 1)
                ]
                for a in range(taps):
                    products = [grads[row] * lines[row + a] for row in range(group)]
                    while len(products) > 1:
                        products = [x + y for x, y in zip(products[::2], products[1::2])]
                    sums[a] = sums[a] + products[0].astype(F32)
        for a in range(taps):
            target[b, pl.ds(a, 1), lanes] = jnp.sum(sums[a], axis=0, keepdims=True)
        return carry

    lax.fori_loop(0, taps, over, 0)


ORDER = (0, 3, 1, 2)


def correct(padded, flank, part, kern_ref, side, taps, flipped, target):
    pitch = pitch_of(side)
    margin = taps // 2
    lanes = pl.ds(part * LANES, LANES)

    def weight(a, b):
        if flipped:
            a, b = taps - 1 - a, taps - 1 - b
        return kern_ref[a, pl.ds(b, 1), lanes]

    for far in range(2):
        for out in range(margin):
            row = side - margin + out if far else out
            total = jnp.zeros((side, LANES), F32)
            for near in range(margin):
                up = margin + side + near - row if far else near - row
                if 0 <= up < taps:
                    start = (margin + side + near if far else near) * pitch + LEAD - margin
                    for col in range(taps):
                        total = total + weight(up, col) * padded[part, pl.ds(start + col, side), :]
            target[part, pl.ds(row * side, side), :] += total
        for out in range(margin):
            col = side - margin + out if far else out
            total = jnp.zeros((side, LANES), F32)
            for near in range(margin):
                over = margin + side + near - col if far else near - col
                if 0 <= over < taps:
                    for row in range(taps):
                        line = flank[far, near, part, pl.ds(LEAD - margin + row, side), :]
                        total = total + weight(row, over) * line
            at = pl.ds(col, side, stride=side)
            target[part, at, :] = target[part, at, :] + total


def contract_rows(left, right):
    return lax.dot_general(left, right, (((0,), (0,)), ((), ())), preferred_element_type=F32)


def contract_cols(left, right):
    return lax.dot_general(left, right, (((1,), (1,)), ((), ())), preferred_element_type=F32)


def whole_kernel(
    side,
    taps,
    members,
    tiles,
    chunk,
    block,
    links_ref,
    state_hbm,
    kern_ref,
    cbias_ref,
    gain_ref,
    shift_ref,
    bin_ref,
    bout_ref,
    scale_ref,
    cot_hbm,
    win_hbm,
    wout_hbm,
    new_hbm,
    sgrad_hbm,
    out_ref,
    sout_ref,
    padded,
    gpad,
    flank,
    packed,
    gpacked,
    taps_ref,
    gkern_ref,
    mixed_ref,
    inv_ref,
    normed_ref,
    low_ref,
    act_ref,
    glow_ref,
    gact_ref,
    gmix_ref,
    gbin_ref,
    gch_ref,
    state_ref,
    cot_ref,
    win_ref,
    wout_ref,
    new_ref,
    sgrad_ref,
    send,
    recv,
    gsend,
    grecv,
    big,
    core_in,
    a_x,
    b_x,
    c_x,
    d_x,
    a_y,
    b_y,
    c_y,
    d_y,
    e_out,
    f_in,
    own,
    s_pack,
    s_send,
    sm_in,
    st_out,
    st_in,
    s_own,
    load_sem,
    halo_sem,
    ghalo_sem,
    core_sem,
    bx_sem,
    dx_sem,
    by_sem,
    dy_sem,
    f_send,
    f_recv,
    g_sem,
    sm_sem,
    st_sem,
    sg_sem,
    store_sem,
):
    margin = taps // 2
    parts = padded.shape[0]
    cells = side * side
    groups = side // 4
    pitch = pitch_of(side)
    hidden = win_ref.shape[1]
    width = win_ref.shape[0]
    fourth = hidden // 4
    chunks = 2
    per = tiles // chunks
    spots = members // 2
    rows = hidden // (tiles * members)
    member = lax.axis_index("member")
    tile = lax.axis_index("tile")
    core = lax.rem(member, 2)
    cross = member // 2
    odd = lax.rem(tile, 2)
    quarter = tiles // 4
    half_per = per // 2
    along = [lax.rem(tile + 2 * k, tiles) for k in range(1, tiles // 2)]
    mates = [lax.rem(member + k, members) for k in range(1, members)]
    peers = [lax.rem(tile + k, tiles) for k in range(1, tiles)]
    barrier = pltpu.get_barrier_semaphore()
    for mate in mates:
        pl.semaphore_signal(barrier, inc=1, device_id={"member": mate}, device_id_type=MESH)
    for peer in peers:
        pl.semaphore_signal(barrier, inc=1, device_id={"tile": peer}, device_id_type=MESH)
    moves = [(state_hbm, state_ref), (cot_hbm, cot_ref)]
    for k, source in enumerate(ORDER):
        old, new = pl.ds(source * fourth, fourth), pl.ds(k * fourth, fourth)
        moves.append((win_hbm.at[:, old], win_ref.at[:, new]))
        moves.append((wout_hbm.at[old, :], wout_ref.at[new, :]))
    loads = [
        pltpu.make_async_copy(source, target, load_sem.at[k])
        for k, (source, target) in enumerate(moves)
    ]
    for load in loads:
        load.start()

    loads[0].wait()

    def center(part, row):
        at = pl.ds(pl.multiple_of(row * side, side), side)
        return state_ref[at, pl.ds(part * LANES, LANES)].astype(F32)

    place(padded, side, margin, center)
    swap_halo(
        padded, side, margin, links_ref, send, recv, halo_sem, tiles,
        lambda: pl.semaphore_wait(barrier, members + tiles - 2),
    )

    def forward_emit(part):
        bias = cbias_ref[pl.ds(part * LANES, LANES)].reshape(1, LANES)

        def emit(start, value):
            mixed_ref[part, pl.ds(start, side), :] = value + bias

        return emit

    for part in range(parts):
        convolve_wide(padded, part, kern_ref, side, taps, forward_emit(part))
    spread_taps(kern_ref, taps_ref, taps)
    gbin_ref[...] = jnp.zeros_like(gbin_ref)
    gch_ref[...] = jnp.zeros_like(gch_ref)
    for load in loads[1:]:
        load.wait()

    def cotangent_step(r, carry):
        at = pl.ds(pl.multiple_of(r * block, block), block)
        grad_branch = scale_ref[...].reshape(1, -1) * cot_ref[at, :].astype(F32)
        low = grad_branch.astype(BF16)
        low_ref[at, :] = low
        gch_ref[3:4, :] += jnp.sum(grad_branch, axis=0, keepdims=True)
        for h in range(2):
            here = slice(h * chunk, (h + 1) * chunk)
            gact_ref[at, here] = contract_cols(low, wout_ref[here, :])
        return carry

    lax.fori_loop(0, cells // block, cotangent_step, 0)
    wait_halo(send, recv, halo_sem, tiles)
    take_halo(padded, side, margin, links_ref, recv, tiles, flank)
    for part in range(parts):
        correct(padded, flank, part, kern_ref, side, taps, False, mixed_ref)

    def prepare_cells(at):
        mixed = jnp.concatenate([mixed_ref[part, at, :] for part in range(parts)], axis=1)
        centered = mixed - jnp.mean(mixed, axis=1, keepdims=True)
        variance = jnp.mean(centered * centered, axis=1, keepdims=True)
        inv_std = lax.rsqrt(variance + EPSILON)
        norm_hat = centered * inv_std
        for part in range(parts):
            mixed_ref[part, at, :] = norm_hat[:, part * LANES : (part + 1) * LANES]
        inv_ref[at, :] = jnp.broadcast_to(inv_std, (block, LANES))
        normed_ref[at, :] = (norm_hat * gain_ref[...].reshape(1, -1) + shift_ref[...].reshape(1, -1)).astype(BF16)

    def finish_cells(at, branch, grad_normed):
        gain = gain_ref[...].reshape(1, -1)
        branch = branch + bout_ref[...].reshape(1, -1)
        scaled_branch = scale_ref[...].reshape(1, -1) * branch
        new_ref[at, :] = (state_ref[at, :].astype(F32) + scaled_branch).astype(BF16)
        norm_hat = jnp.concatenate([mixed_ref[part, at, :] for part in range(parts)], axis=1)
        scaled = grad_normed * gain
        inner = (
            scaled
            - jnp.mean(scaled, axis=1, keepdims=True)
            - norm_hat * jnp.mean(scaled * norm_hat, axis=1, keepdims=True)
        )
        inv_std = inv_ref[at, :]
        for part in range(parts):
            lanes = slice(part * LANES, (part + 1) * LANES)
            grad_mixed = inv_std * inner[:, lanes]
            gmix_ref[part, at, :] = grad_mixed
            gch_ref[0:1, lanes] += jnp.sum(grad_mixed, axis=0, keepdims=True)
        gch_ref[1:2, :] += jnp.sum(grad_normed * norm_hat, axis=0, keepdims=True)
        gch_ref[2:3, :] += jnp.sum(grad_normed, axis=0, keepdims=True)
        gch_ref[4:5, :] += jnp.sum(cot_ref[at, :].astype(F32) * branch, axis=0, keepdims=True)

    def exchange_core(h):
        return [
            prepare(
                big.at[h, :, :, :, :, 1 - core], core_in.at[h], core_sem, h,
                member=cross * 2 + 1 - core,
            )
        ]

    def across(source, target, sems, h):
        copies = []
        for k in range(1, spots):
            spot = lax.rem(cross + k, spots)
            copies.append(
                prepare(
                    source.at[h, spot], target.at[h, k - 1], sems, h * (spots - 1) + k - 1,
                    member=spot * 2 + core,
                )
            )
        return copies

    def sideways(source, target, sems, h):
        return [prepare(source.at[h, 1 - odd], target.at[h], sems, h, tile=tile + 1 - 2 * odd)]

    def first_hop(h):
        return across(a_x, b_x, bx_sem, h) + sideways(a_y, b_y, by_sem, h)

    def second_hop(h):
        return sideways(c_y, d_y, dy_sem, h) + across(c_x, d_x, dx_sem, h)

    def spot_of(other):
        place = lax.div(other, 2)
        half = quarter // 2
        outer = jnp.logical_or(place < half, place >= 3 * half)
        at = jnp.where(place < half, place, jnp.where(outer, place - 2 * half, place - half))
        return outer, at

    def third_hop(h, k):
        other = along[k]
        outer, at = spot_of(other)
        return pltpu.make_async_remote_copy(
            src_ref=e_out.at[h, jnp.clip(at, 0, half_per - 1)],
            dst_ref=f_in.at[k],
            send_sem=f_send.at[h, k],
            recv_sem=f_recv.at[k],
            device_id={"tile": other},
            device_id_type=MESH,
        )

    def goes(h, k):
        outer, at = spot_of(along[k])
        return outer if h == 0 else jnp.logical_not(outer)

    def start_first(h):
        for copy in exchange_core(h):
            copy.wait()

        def add(j, carry):
            for y in range(2):
                for x in range(spots):
                    for kind in range(2):
                        value = big[h, kind, j, y, x, core].astype(F32) + core_in[h, kind, j, y, x].astype(F32)
                        if kind == 0:
                            a_x[h, x, j, y] = value.astype(BF16)
                        else:
                            a_y[h, y, j, x] = value.astype(BF16)
            return carry

        lax.fori_loop(0, half_per, add, 0)
        for copy in first_hop(h):
            copy.start()

    def start_second(h):
        for copy in first_hop(h):
            copy.wait()

        def add(j, carry):
            for y in range(2):
                value = a_x[h, cross, j, y].astype(F32)
                for k in range(spots - 1):
                    value = value + b_x[h, k, j, y].astype(F32)
                c_y[h, y, j] = value.astype(BF16)
            for x in range(spots):
                value = a_y[h, odd, j, x].astype(F32) + b_y[h, j, x].astype(F32)
                c_x[h, x, j] = value.astype(BF16)
            return carry

        lax.fori_loop(0, half_per, add, 0)
        for copy in second_hop(h):
            copy.start()

    def start_third(h):
        for copy in second_hop(h):
            copy.wait()

        def add(j, carry):
            value = c_y[h, odd, j].astype(F32) + d_y[h, j].astype(F32)
            e_out[h, j, 0] = value.astype(BF16)
            value = c_x[h, cross, j].astype(F32)
            for k in range(spots - 1):
                value = value + d_x[h, k, j].astype(F32)
            e_out[h, j, 1] = value.astype(BF16)
            return carry

        lax.fori_loop(0, half_per, add, 0)
        for k in range(len(along)):

            @pl.when(goes(h, k))
            def _():
                third_hop(h, k).start()

    def bias_of(h):
        quarters = [bin_ref[pl.ds(k * fourth, fourth)].reshape(1, fourth) for k in ORDER[2 * h : 2 * h + 2]]
        return jnp.concatenate(quarters, axis=1)

    def mlp(h, r):
        at = pl.ds(pl.multiple_of(r * block, block), block)
        if h == 0:
            prepare_cells(at)
        here = slice(h * chunk, (h + 1) * chunk)
        win = win_ref[:, here]
        pre = jnp.dot(normed_ref[at, :], win, preferred_element_type=F32) + bias_of(h)
        square = pre * pre
        tanh_value = jnp.tanh(GELU_SCALE * pre * (1.0 + GELU_CUBIC * square))
        half = 0.5 * (1.0 + tanh_value)
        activation = (pre * half).astype(BF16)
        slope = half + (0.5 * GELU_SCALE) * pre * (1.0 - tanh_value * tanh_value) * (
            1.0 + 3.0 * GELU_CUBIC * square
        )
        grad_pre = gact_ref[at, here] * slope
        grad_low = grad_pre.astype(BF16)
        act_ref[at, here] = activation
        glow_ref[at, here] = grad_low
        gbin_ref[:, here] += jnp.sum(grad_pre, axis=0, keepdims=True)

    def close_cells(r):
        at = pl.ds(pl.multiple_of(r * block, block), block)
        branch = jnp.dot(act_ref[at, :], wout_ref[...], preferred_element_type=F32)
        grad_normed = contract_cols(glow_ref[at, :], win_ref[...])
        finish_cells(at, branch, grad_normed)

    def weights(h):
        for kind, (left, right) in enumerate([(glow_ref, normed_ref), (act_ref, low_ref)]):
            value = contract_rows(left[:, h * chunk : (h + 1) * chunk], right[...])
            for index in range(per * members):
                j, y = index // members // 2, index // members % 2
                x, c = index % members // 2, index % 2
                big[h, kind, j, y, x, c] = value[index * rows : (index + 1) * rows].astype(BF16)
        for copy in exchange_core(h):
            copy.start()

    def inner_step(r, carry):
        mlp(0, r)
        return carry

    def outer_step(r, carry):
        mlp(1, r)

        @pl.when(r == 0)
        def _():
            start_first(0)

        return carry

    def close_step(r, carry):
        close_cells(r)

        @pl.when(r == 0)
        def _():
            start_second(0)
            start_first(1)

        return carry

    lax.fori_loop(0, cells // block, inner_step, 0)
    weights(0)
    lax.fori_loop(0, cells // block, outer_step, 0)
    weights(1)
    lax.fori_loop(0, cells // block, close_step, 0)
    new_copy = pltpu.make_async_copy(new_ref, new_hbm, store_sem.at[0])
    new_copy.start()

    def gcenter(part, row):
        at = pl.ds(pl.multiple_of(row * side, side), side)
        return gmix_ref[part, at, :].astype(BF16).astype(F32)

    place(gpad, side, margin, gcenter)
    swap_halo(
        gpad, side, margin, links_ref, gsend, grecv, ghalo_sem, tiles, lambda: None
    )
    lines = s_pack.shape[1]
    s_pack[...] = jnp.zeros_like(s_pack)
    first = taps * taps
    extra = gbin_ref.shape[1] // width
    for row in range(extra):
        at = first + row
        s_pack[at // lines, pl.ds(at % lines, 1), :] = gbin_ref[:, pl.ds(ORDER.index(row) * width, width)]
    for row in range(5):
        at = first + extra + row
        s_pack[at // lines, pl.ds(at % lines, 1), :] = gch_ref[pl.ds(row, 1), :]

    def emit(part, at, value):
        mixed_ref[part, at, :] = value

    regroup(padded, packed, side, margin)
    regroup(gpad, gpacked, side, margin)
    start_third(0)
    kernel_grad(packed, gpacked, gkern_ref, 0, side, taps)
    kernel_grad(packed, gpacked, gkern_ref, 1, side, taps)
    start_second(1)
    kernel_grad(packed, gpacked, gkern_ref, 2, side, taps)
    for up in range(taps):
        for col in range(taps):
            at = up * taps + col
            line = gkern_ref[col, up : up + 1, :]
            s_pack[at // lines, pl.ds(at % lines, 1), :] = line[:, :width] + line[:, width:]
    s_send[...] = s_pack[...].astype(BF16)
    small = [
        remote(s_send.at[mate], sm_in.at[k], sm_sem, k, member=mate) for k, mate in enumerate(mates)
    ]
    convolve(gpacked, taps_ref, side, taps, emit, 0, 1)
    convolve(gpacked, taps_ref, side, taps, emit, 1, 2)
    for copy in small:
        copy.wait()
    total = s_pack[member]
    for k in range(members - 1):
        total = total + sm_in[k].astype(F32)
    st_out[...] = total.astype(BF16)
    st_in[tile] = total.astype(BF16)
    small = [
        remote(st_out, st_in.at[tile], st_sem, k, tile=peer) for k, peer in enumerate(peers)
    ]
    start_third(1)
    convolve(gpacked, taps_ref, side, taps, emit, 2, 3)
    wait_halo(gsend, grecv, ghalo_sem, tiles)
    take_halo(gpad, side, margin, links_ref, grecv, tiles, flank)
    for part in range(parts):
        lanes = pl.ds(part * LANES, LANES)
        correct(gpad, flank, part, kern_ref, side, taps, True, mixed_ref)

        def close(row, carry):
            at = pl.ds(pl.multiple_of(row * LANES, LANES), LANES)
            sgrad_ref[at, lanes] = (cot_ref[at, lanes].astype(F32) + mixed_ref[part, at, :]).astype(BF16)
            return carry

        lax.fori_loop(0, cells // LANES, close, 0)
    store = pltpu.make_async_copy(sgrad_ref, sgrad_hbm, store_sem.at[1])
    store.start()
    for copy in small:
        copy.wait()
    total = st_in[0].astype(F32)
    for k in range(1, tiles):
        total = total + st_in[k].astype(F32)
    s_own[...] = total
    sout_ref[member] = total
    small = [
        remote(s_own, sout_ref.at[member], sg_sem, k, member=mate) for k, mate in enumerate(mates)
    ]
    for k in range(len(along)):
        third_hop(0, k).wait_recv()
        for h in range(chunks):

            @pl.when(goes(h, k))
            def _():
                third_hop(h, k).wait_send()

    outer, at = spot_of(tile)
    for h in range(chunks):

        @pl.when(outer if h == 0 else jnp.logical_not(outer))
        def _():
            for kind in range(2):
                value = e_out[h, jnp.clip(at, 0, half_per - 1), kind].astype(F32)
                for k in range(len(along)):
                    value = value + f_in[k, kind].astype(F32)
                own[kind] = value.astype(BF16)

    out_ref[member] = own[...]
    back = [
        remote(own, out_ref.at[member], g_sem, k, member=mate) for k, mate in enumerate(mates)
    ]
    for copy in small + back:
        copy.wait()
    new_copy.wait()
    store.wait()


def run_whole(links, state, cot, kern, vectors, w_in, w_out, side, members, tiles, chunk=768, block=512):
    cells, width = state.shape
    hidden = w_in.shape[1]
    taps = kern.shape[0]
    margin = taps // 2
    chunks = 2
    half = tiles // chunks // 2
    spots = members // 2
    rows = hidden // (tiles * members)
    piece = lambda *n: pltpu.VMEM((chunks, *n, rows, width), BF16)
    used = taps * taps + hidden // width + 5
    lines = 16 * (-(-used // (16 * members)))
    others = max(spots - 1, 1)
    parts = width // LANES
    spread = spread_of(side, margin)
    dma = lambda *n: pltpu.SemaphoreType.DMA(n)
    strips = (len(OFFSETS), margin, side, width)
    anywhere = pl.BlockSpec(memory_space=pl.ANY)
    return pl.pallas_call(
        functools.partial(whole_kernel, side, taps, members, tiles, chunk, block),
        in_specs=[smem_spec(), anywhere] + [vmem_spec()] * 7 + [anywhere] * 3,
        out_specs=[anywhere] * 2 + [vmem_spec()] * 2,
        out_shape=[
            jax.ShapeDtypeStruct((cells, width), BF16),
            jax.ShapeDtypeStruct((cells, width), BF16),
            jax.ShapeDtypeStruct((members, 2, rows, width), BF16),
            jax.ShapeDtypeStruct((members, lines, width), F32),
        ],
        scratch_shapes=[
            pltpu.VMEM((parts, spread, LANES), F32),
            pltpu.VMEM((parts, spread, LANES), F32),
            pltpu.VMEM((2, margin, parts, pitch_of(side), LANES), F32),
            pltpu.VMEM((packed_of(side, margin), 8, 2 * width), BF16),
            pltpu.VMEM((packed_of(side, margin), 8, 2 * width), BF16),
            pltpu.VMEM((taps * taps, 8, 2 * width), BF16),
            pltpu.VMEM((taps, 8, 2 * width), F32),
            pltpu.VMEM((parts, cells, LANES), F32),
            pltpu.VMEM((cells, LANES), F32),
            pltpu.VMEM((cells, width), BF16),
            pltpu.VMEM((cells, width), BF16),
            pltpu.VMEM((cells, hidden), BF16),
            pltpu.VMEM((cells, hidden), BF16),
            pltpu.VMEM((cells, hidden), F32),
            pltpu.VMEM((parts, cells, LANES), F32),
            pltpu.VMEM((1, hidden), F32),
            pltpu.VMEM((8, width), F32),
            pltpu.VMEM((cells, width), BF16),
            pltpu.VMEM((cells, width), BF16),
            pltpu.VMEM((width, hidden), BF16),
            pltpu.VMEM((hidden, width), BF16),
            pltpu.VMEM((cells, width), BF16),
            pltpu.VMEM((cells, width), BF16),
            pltpu.VMEM(strips, BF16),
            pltpu.VMEM(strips, BF16),
            pltpu.VMEM(strips, BF16),
            pltpu.VMEM(strips, BF16),
            piece(2, half, 2, spots, 2),
            piece(2, half, 2, spots),
            piece(spots, half, 2),
            piece(others, half, 2),
            piece(spots, half),
            piece(others, half),
            piece(2, half, spots),
            piece(half, spots),
            piece(2, half),
            piece(half),
            piece(half, 2),
            pltpu.VMEM((tiles // 2 - 1, 2, rows, width), BF16),
            pltpu.VMEM((2, rows, width), BF16),
            pltpu.VMEM((members, lines, width), F32),
            pltpu.VMEM((members, lines, width), BF16),
            pltpu.VMEM((members - 1, lines, width), BF16),
            pltpu.VMEM((lines, width), BF16),
            pltpu.VMEM((tiles, lines, width), BF16),
            pltpu.VMEM((lines, width), F32),
            dma(10),
            dma(2, len(OFFSETS)),
            dma(2, len(OFFSETS)),
            dma(2, chunks),
            dma(2, chunks * others),
            dma(2, chunks * others),
            dma(2, chunks),
            dma(2, chunks),
            dma(chunks, tiles // 2 - 1),
            dma(tiles // 2 - 1),
            dma(2, members - 1),
            dma(2, members - 1),
            dma(2, tiles - 1),
            dma(2, members - 1),
            dma(2),
        ],
        compiler_params=remote_params(0),
        name="whole",
    )(links, state, kern, *vectors, cot, w_in, w_out)


def finish_kernel(taps, factor, big_hbm, small_hbm, new_hbm, sgrad_hbm, *rest):
    outs, kept = rest[:7], rest[7:]
    big_ref, small_ref, held, win_ref, wout_ref, kern_ref, bin_ref, ch_ref, in_sem, out_sem, sems = kept
    members, _, rows, width = big_ref.shape
    lines = small_ref.shape[1]
    pieces = held.shape[1]
    size = held.shape[2]
    first_in = [
        pltpu.make_async_copy(source, target, in_sem.at[k])
        for k, (source, target) in enumerate([(big_hbm, big_ref), (small_hbm, small_ref)])
    ]
    inward, outward = [], []
    for k, (source, target) in enumerate([(new_hbm, outs[0]), (sgrad_hbm, outs[1])]):
        for piece in range(pieces):
            at = pl.ds(piece * size, size)
            here = held.at[k, piece]
            inward.append(pltpu.make_async_copy(source.at[at, :], here, sems.at[0, k, piece]))
            outward.append(pltpu.make_async_copy(here, target.at[at, :], sems.at[1, k, piece]))
    last_out = [
        pltpu.make_async_copy(source, target, out_sem.at[k])
        for k, (source, target) in enumerate(
            zip((win_ref, wout_ref, kern_ref, bin_ref, ch_ref), outs[2:])
        )
    ]
    for copy in first_in + inward:
        copy.start()
    first_in[0].wait()
    for m in range(members):
        win_ref[pl.ds(m * rows, rows), :] = big_ref[m, 0].astype(F32) * factor
        wout_ref[pl.ds(m * rows, rows), :] = big_ref[m, 1].astype(F32) * factor
    for copy in last_out[:2]:
        copy.start()
    for come, go in zip(inward, outward):
        come.wait()
        go.start()
    first_in[1].wait()

    def line(at):
        return small_ref[at // lines, pl.ds(at % lines, 1), :] * factor

    for at in range(taps * taps):
        kern_ref[at // taps, pl.ds(at % taps, 1), :] = line(at)
    first = taps * taps
    extra = bin_ref.shape[0] // width
    for at in range(extra):
        bin_ref[pl.ds(at * width, width)] = line(first + at).reshape(width)
    for at in range(5):
        ch_ref[pl.ds(at, 1), :] = line(first + extra + at)
    for copy in last_out[2:]:
        copy.start()
    for copy in outward + last_out:
        copy.wait()


def finish(big, small, new, sgrad, share, taps, hidden, factor, pieces=2):
    width = big.shape[3]
    shapes = [(share, width), (share, width), (taps, taps, width), (hidden,), (5, width)]
    anywhere = pl.BlockSpec(memory_space=pl.ANY)
    return pl.pallas_call(
        functools.partial(finish_kernel, taps, factor),
        in_specs=[anywhere] * 4,
        out_specs=[anywhere] * 7,
        out_shape=[jax.ShapeDtypeStruct(new.shape, BF16)] * 2
        + [jax.ShapeDtypeStruct(shape, F32) for shape in shapes],
        scratch_shapes=[
            pltpu.VMEM(big.shape, BF16),
            pltpu.VMEM(small.shape, F32),
            pltpu.VMEM((2, pieces, new.shape[0] // pieces, width), BF16),
        ]
        + [pltpu.VMEM(shape, F32) for shape in shapes]
        + [
            pltpu.SemaphoreType.DMA((2,)),
            pltpu.SemaphoreType.DMA((5,)),
            pltpu.SemaphoreType.DMA((2, 2, pieces)),
        ],
        compiler_params=local_params(),
        name="finish",
    )(big, small, new, sgrad)


def body(
    state,
    cotangent,
    neighbors,
    kernel,
    conv_bias,
    norm_gain,
    norm_shift,
    w_in,
    bias_in,
    w_out,
    bias_out,
    layer_scale,
):
    side, width = state.shape[2], state.shape[4]
    cells = side * side
    center = state.reshape(cells, width)
    cot = cotangent.reshape(cells, width)
    hidden = w_in.shape[1]
    taps = kernel.shape[0]
    tiles = lax.axis_size("tile")
    members = lax.axis_size("member")
    vectors = (conv_bias, norm_gain, norm_shift, bias_in, bias_out, layer_scale)
    new_tile, state_grad, big, small = run_whole(
        neighbors, center, cot, kernel, vectors, w_in, w_out, side, members, tiles
    )
    share = hidden // tiles
    factor = 1.0 / math.sqrt(members * tiles * cells)
    new_tile, state_grad, win_share, *shares = finish(
        big, small, new_tile, state_grad, share, taps, hidden, factor
    )
    return (
        new_tile.reshape(state.shape),
        state_grad.reshape(state.shape),
        win_share.T,
        *shares,
    )


def solution(mesh):
    tiled = P("member", "tile", None, None, None)
    in_specs = (tiled, tiled) + (P(),) * 10
    out_specs = (tiled, tiled, P(None, "tile"), P("tile", None), P(), P(), P())
    return jax.shard_map(body, mesh=mesh, in_specs=in_specs, out_specs=out_specs, check_vma=False)
```

```python
import functools
import math

import jax
import jax.numpy as jnp
from jax import lax
from jax.experimental import pallas as pl
from jax.experimental.pallas import tpu as pltpu
from jax.sharding import PartitionSpec as P

OFFSETS = (1, 2, 3, -1, -2, -3)
GELU_SCALE = 0.7978845608028654
GELU_CUBIC = 0.044715
EPSILON = 1e-06
LANES = 128
LEAD = 8
MESH = pl.DeviceIdType.MESH
F32 = jnp.float32
BF16 = jnp.bfloat16
VMEM_LIMIT = 56 << 20


def vmem_spec():
    return pl.BlockSpec(memory_space=pltpu.VMEM)


def smem_spec():
    return pl.BlockSpec(memory_space=pltpu.SMEM)


def local_params():
    return pltpu.CompilerParams(vmem_limit_bytes=VMEM_LIMIT)


def remote_params(ident):
    return pltpu.CompilerParams(
        collective_id=ident, has_side_effects=True, vmem_limit_bytes=VMEM_LIMIT
    )


def pitch_of(side):
    return side + 2 * LEAD


def spread_of(side, margin):
    return (side + 2 * margin) * pitch_of(side)


def place(padded, side, margin, center):
    pitch = pitch_of(side)
    for part in range(padded.shape[0]):

        def clear(row, carry):
            at = pl.ds(pl.multiple_of(row * pitch, 8), pitch)
            padded[part, at, :] = jnp.zeros((pitch, LANES), F32)
            return carry

        lax.fori_loop(0, side + 2 * margin, clear, 0)

        def put(row, carry):
            at = pl.ds(pl.multiple_of((margin + row) * pitch + LEAD, 8), side)
            padded[part, at, :] = center(part, row)
            return carry

        lax.fori_loop(0, side, put, 0)


def around(tile, count):
    takers = [lax.rem(tile + offset + count, count) for offset in OFFSETS]
    givers = [lax.rem(tile - offset + count, count) for offset in OFFSETS]
    return takers, givers


def pack(padded, side, margin, want, send_ref):
    pitch = pitch_of(side)
    edge = side - margin
    for part in range(padded.shape[0]):
        lanes = pl.ds(part * LANES, LANES)
        for k in range(margin):
            low = (margin + k) * pitch + LEAD
            high = (margin + edge + k) * pitch + LEAD
            first = margin * pitch + LEAD
            lines = [
                padded[part, pl.ds(low, side), :],
                padded[part, pl.ds(high, side), :],
                padded[part, pl.ds(first + k, side, stride=pitch), :],
                padded[part, pl.ds(first + edge + k, side, stride=pitch), :],
            ]
            lines = lines + [
                jnp.concatenate([lines[0][:8]] * (side // 8), axis=0),
                jnp.concatenate([lines[0][side - 8 :]] * (side // 8), axis=0),
                jnp.concatenate([lines[1][:8]] * (side // 8), axis=0),
                jnp.concatenate([lines[1][side - 8 :]] * (side // 8), axis=0),
            ]
            for slot in range(len(OFFSETS)):
                line = lines[7]
                for way in range(7):
                    line = jnp.where(want[slot][way], lines[way], line)
                send_ref[slot, k, :, lanes] = line.astype(BF16)


def unpack(padded, side, margin, have, recv_ref, flank):
    pitch = pitch_of(side)
    for part in range(padded.shape[0]):
        lanes = pl.ds(part * LANES, LANES)
        for k in range(margin):
            lines = [recv_ref[slot, k, :, lanes].astype(F32) for slot in range(len(OFFSETS))]
            for way in range(8):
                size = side if way < 4 else 8
                line = jnp.zeros((size, LANES), F32)
                for slot in range(len(OFFSETS)):
                    line = jnp.where(have[slot][way], lines[slot][:size], line)
                if way == 0:
                    at = pl.ds((margin + side + k) * pitch + LEAD, side)
                elif way == 1:
                    at = pl.ds(k * pitch + LEAD, side)
                elif way == 2:
                    at = pl.ds(margin * pitch + LEAD + side + k, side, stride=pitch)
                elif way == 3:
                    at = pl.ds(margin * pitch + LEAD - margin + k, side, stride=pitch)
                else:
                    row = margin + side + k if way in (4, 5) else k
                    at = pl.ds(row * pitch + (LEAD + side if way in (4, 6) else LEAD - 8), 8)
                padded[part, at, :] = line
                if way in (2, 3):
                    far = 3 - way
                    blank = jnp.zeros((LEAD, LANES), F32)
                    flank[far, k, part, pl.ds(0, LEAD), :] = blank
                    flank[far, k, part, pl.ds(LEAD, side), :] = line
                    flank[far, k, part, pl.ds(LEAD + side, LEAD), :] = blank


def prepare(source, target, sems, slot, **device):
    return pltpu.make_async_remote_copy(
        src_ref=source,
        dst_ref=target,
        send_sem=sems.at[0, slot],
        recv_sem=sems.at[1, slot],
        device_id=device,
        device_id_type=MESH,
    )


def remote(source, target, sems, slot, **device):
    copy = prepare(source, target, sems, slot, **device)
    copy.start()
    return copy


def strip_to(slot, send_ref, recv_ref, sems, count):
    tile = lax.axis_index("tile")
    takers, _ = around(tile, count)
    return prepare(send_ref.at[slot], recv_ref.at[slot], sems, slot, tile=takers[slot])


def idle(slot, count, receiving):
    tile = lax.axis_index("tile")
    if abs(OFFSETS[slot]) < 3:
        return None
    low = (OFFSETS[slot] > 0) == receiving
    ends = (0, 2) if low else (count - 3, count - 1)
    return jnp.logical_or(tile == ends[0], tile == ends[1])


def unless(condition, act):
    if condition is None:
        act()
    else:
        pl.when(jnp.logical_not(condition))(act)


def swap_halo(padded, side, margin, links_ref, send_ref, recv_ref, sems, count, ready):
    tile = lax.axis_index("tile")
    takers, _ = around(tile, count)
    want = [[links_ref[taker, way] == tile for way in range(8)] for taker in takers]
    pack(padded, side, margin, want, send_ref)
    ready()
    for slot in range(len(OFFSETS)):
        unless(
            idle(slot, count, False),
            lambda slot=slot: strip_to(slot, send_ref, recv_ref, sems, count).start(),
        )


def wait_halo(send_ref, recv_ref, sems, count):
    for slot in range(len(OFFSETS)):
        copy = strip_to(slot, send_ref, recv_ref, sems, count)
        unless(idle(slot, count, False), copy.wait_send)
        unless(idle(slot, count, True), copy.wait_recv)


def take_halo(padded, side, margin, links_ref, recv_ref, count, flank):
    tile = lax.axis_index("tile")
    _, givers = around(tile, count)
    have = [[links_ref[tile, way] == giver for way in range(8)] for giver in givers]
    unpack(padded, side, margin, have, recv_ref, flank)


def packed_of(side, margin):
    return (side // 2 + 2 * margin) * (side // 8 + 2 * margin)


def regroup(padded, packed, side, margin):
    pitch = pitch_of(side)
    step = side // 8
    columns = step + 2 * margin

    def row(up, carry):
        for col in range(columns):
            values = [
                padded[
                    part,
                    pl.ds((side // 2 * half + up) * pitch + LEAD - margin + col, 8, stride=step),
                    :,
                ]
                for half in range(2)
                for part in range(padded.shape[0])
            ]
            packed[up * columns + col] = jnp.concatenate(values, axis=1).astype(BF16)
        return carry

    lax.fori_loop(0, side // 2 + 2 * margin, row, 0)


def spread_taps(kern_ref, taps_ref, taps):
    for a in range(taps):
        for b in range(taps):
            line = kern_ref[a, pl.ds(b, 1), :]
            line = jnp.concatenate([line, line], axis=1)
            taps_ref[a * taps + b] = jnp.broadcast_to(line, taps_ref.shape[1:]).astype(BF16)


def convolve_wide(padded, part, kern_ref, side, taps, emit, group=4):
    pitch = pitch_of(side)
    margin = taps // 2
    lanes = pl.ds(part * LANES, LANES)

    def step(index, carry):
        base = index * group
        total = [jnp.zeros((side, LANES), F32) for _ in range(group)]
        for col in range(taps):
            for row in range(group + taps - 1):
                start = (base + row) * pitch
                line = padded[part, pl.ds(start + (LEAD - margin + col), side), :]
                for out in range(group):
                    up = row - out
                    if 0 <= up < taps:
                        total[out] = total[out] + kern_ref[up, pl.ds(col, 1), lanes] * line
        for out in range(group):
            emit(pl.multiple_of((base + out) * side, side), total[out])
        return carry

    lax.fori_loop(0, side // group, step, 0)


def convolve(packed, taps_ref, side, taps, emit, begin, end, group=8):
    step = side // 8
    columns = step + taps - 1
    parts = packed.shape[2] // (2 * LANES)
    for pair in range(begin, end):
        lanes = pl.ds(pair * 2 * LANES, 2 * LANES)

        def block(index, carry):
            base = lax.div(index, step) * group
            col = lax.rem(index, step)
            total = [jnp.zeros((8, 2 * LANES), F32) for _ in range(group)]
            for b in range(taps):
                lines = [
                    packed[(base + row) * columns + col + b, :, lanes]
                    for row in range(group + taps - 1)
                ]
                sums = [None] * group
                for a in range(taps):
                    spot = (taps - 1 - a) * taps + taps - 1 - b
                    weight = taps_ref[spot, :, lanes]
                    for out in range(group):
                        product = weight * lines[out + a]
                        sums[out] = product if a == 0 else sums[out] + product
                for out in range(group):
                    total[out] = total[out] + sums[out].astype(F32)
            for out in range(group):
                for lane in range(2):
                    place = 2 * pair + lane
                    row = side // 2 * (place // parts) + base + out
                    at = pl.ds(row * side + col, 8, stride=step)
                    emit(place % parts, at, total[out][:, lane * LANES : (lane + 1) * LANES])
            return carry

        lax.fori_loop(0, step * (side // 2 // group), block, 0)


def kernel_grad(packed, gpacked, target, pair, side, taps, group=8):
    margin = taps // 2
    step = side // 8
    columns = step + taps - 1
    lanes = pl.ds(pair * 2 * LANES, 2 * LANES)

    def over(b, carry):
        sums = [jnp.zeros((8, 2 * LANES), F32) for _ in range(taps)]
        for col in range(step):
            for base in range(0, side // 2, group):
                grads = [
                    gpacked[(base + row + margin) * columns + col + margin, :, lanes]
                    for row in range(group)
                ]
                lines = [
                    packed[(base + row) * columns + col + b, :, lanes]
                    for row in range(group + taps - 1)
                ]
                for a in range(taps):
                    products = [grads[row] * lines[row + a] for row in range(group)]
                    while len(products) > 1:
                        products = [x + y for x, y in zip(products[::2], products[1::2])]
                    sums[a] = sums[a] + products[0].astype(F32)
        for a in range(taps):
            target[b, pl.ds(a, 1), lanes] = jnp.sum(sums[a], axis=0, keepdims=True)
        return carry

    lax.fori_loop(0, taps, over, 0)


ORDER = (0, 3, 1, 2)


def correct(padded, flank, part, kern_ref, side, taps, flipped, target):
    pitch = pitch_of(side)
    margin = taps // 2
    lanes = pl.ds(part * LANES, LANES)

    def weight(a, b):
        if flipped:
            a, b = taps - 1 - a, taps - 1 - b
        return kern_ref[a, pl.ds(b, 1), lanes]

    for far in range(2):
        for out in range(margin):
            row = side - margin + out if far else out
            total = jnp.zeros((side, LANES), F32)
            for near in range(margin):
                up = margin + side + near - row if far else near - row
                if 0 <= up < taps:
                    start = (margin + side + near if far else near) * pitch + LEAD - margin
                    for col in range(taps):
                        total = total + weight(up, col) * padded[part, pl.ds(start + col, side), :]
            target[part, pl.ds(row * side, side), :] += total
        for out in range(margin):
            col = side - margin + out if far else out
            total = jnp.zeros((side, LANES), F32)
            for near in range(margin):
                over = margin + side + near - col if far else near - col
                if 0 <= over < taps:
                    for row in range(taps):
                        line = flank[far, near, part, pl.ds(LEAD - margin + row, side), :]
                        total = total + weight(row, over) * line
            at = pl.ds(col, side, stride=side)
            target[part, at, :] = target[part, at, :] + total


def contract_rows(left, right):
    return lax.dot_general(left, right, (((0,), (0,)), ((), ())), preferred_element_type=F32)


def contract_cols(left, right):
    return lax.dot_general(left, right, (((1,), (1,)), ((), ())), preferred_element_type=F32)


def whole_kernel(
    side,
    taps,
    members,
    tiles,
    chunk,
    block,
    links_ref,
    state_hbm,
    kern_ref,
    cbias_ref,
    gain_ref,
    shift_ref,
    bin_ref,
    bout_ref,
    scale_ref,
    cot_hbm,
    win_hbm,
    wout_hbm,
    new_hbm,
    sgrad_hbm,
    out_ref,
    sout_ref,
    padded,
    gpad,
    flank,
    packed,
    gpacked,
    taps_ref,
    gkern_ref,
    mixed_ref,
    inv_ref,
    normed_ref,
    low_ref,
    act_ref,
    glow_ref,
    gact_ref,
    gmix_ref,
    gbin_ref,
    gch_ref,
    state_ref,
    cot_ref,
    win_ref,
    wout_ref,
    new_ref,
    sgrad_ref,
    send,
    recv,
    gsend,
    grecv,
    big,
    core_in,
    a_x,
    b_x,
    c_x,
    d_x,
    a_y,
    b_y,
    c_y,
    d_y,
    e_out,
    f_in,
    own,
    s_pack,
    s_send,
    sm_in,
    st_out,
    st_in,
    s_own,
    load_sem,
    halo_sem,
    ghalo_sem,
    core_sem,
    bx_sem,
    dx_sem,
    by_sem,
    dy_sem,
    f_send,
    f_recv,
    g_sem,
    sm_sem,
    st_sem,
    sg_sem,
    store_sem,
):
    margin = taps // 2
    parts = padded.shape[0]
    cells = side * side
    groups = side // 4
    pitch = pitch_of(side)
    hidden = win_ref.shape[1]
    width = win_ref.shape[0]
    fourth = hidden // 4
    chunks = 2
    per = tiles // chunks
    spots = members // 2
    rows = hidden // (tiles * members)
    member = lax.axis_index("member")
    tile = lax.axis_index("tile")
    core = lax.rem(member, 2)
    cross = member // 2
    odd = lax.rem(tile, 2)
    quarter = tiles // 4
    half_per = per // 2
    along = [lax.rem(tile + 2 * k, tiles) for k in range(1, tiles // 2)]
    mates = [lax.rem(member + k, members) for k in range(1, members)]
    peers = [lax.rem(tile + k, tiles) for k in range(1, tiles)]
    barrier = pltpu.get_barrier_semaphore()
    for mate in mates:
        pl.semaphore_signal(barrier, inc=1, device_id={"member": mate}, device_id_type=MESH)
    for peer in peers:
        pl.semaphore_signal(barrier, inc=1, device_id={"tile": peer}, device_id_type=MESH)
    moves = [(state_hbm, state_ref), (cot_hbm, cot_ref)]
    for k, source in enumerate(ORDER):
        old, new = pl.ds(source * fourth, fourth), pl.ds(k * fourth, fourth)
        moves.append((win_hbm.at[:, old], win_ref.at[:, new]))
        moves.append((wout_hbm.at[old, :], wout_ref.at[new, :]))
    loads = [
        pltpu.make_async_copy(source, target, load_sem.at[k])
        for k, (source, target) in enumerate(moves)
    ]
    for load in loads:
        load.start()

    loads[0].wait()

    def center(part, row):
        at = pl.ds(pl.multiple_of(row * side, side), side)
        return state_ref[at, pl.ds(part * LANES, LANES)].astype(F32)

    place(padded, side, margin, center)
    swap_halo(
        padded, side, margin, links_ref, send, recv, halo_sem, tiles,
        lambda: pl.semaphore_wait(barrier, members + tiles - 2),
    )

    def forward_emit(part):
        bias = cbias_ref[pl.ds(part * LANES, LANES)].reshape(1, LANES)

        def emit(start, value):
            mixed_ref[part, pl.ds(start, side), :] = value + bias

        return emit

    for part in range(parts):
        convolve_wide(padded, part, kern_ref, side, taps, forward_emit(part))
    spread_taps(kern_ref, taps_ref, taps)
    gbin_ref[...] = jnp.zeros_like(gbin_ref)
    gch_ref[...] = jnp.zeros_like(gch_ref)
    for load in loads[1:]:
        load.wait()

    def cotangent_step(r, carry):
        at = pl.ds(pl.multiple_of(r * block, block), block)
        grad_branch = scale_ref[...].reshape(1, -1) * cot_ref[at, :].astype(F32)
        low = grad_branch.astype(BF16)
        low_ref[at, :] = low
        gch_ref[3:4, :] += jnp.sum(grad_branch, axis=0, keepdims=True)
        for h in range(2):
            here = slice(h * chunk, (h + 1) * chunk)
            gact_ref[at, here] = contract_cols(low, wout_ref[here, :])
        return carry

    lax.fori_loop(0, cells // block, cotangent_step, 0)
    wait_halo(send, recv, halo_sem, tiles)
    take_halo(padded, side, margin, links_ref, recv, tiles, flank)
    for part in range(parts):
        correct(padded, flank, part, kern_ref, side, taps, False, mixed_ref)

    def prepare_cells(at):
        mixed = jnp.concatenate([mixed_ref[part, at, :] for part in range(parts)], axis=1)
        centered = mixed - jnp.mean(mixed, axis=1, keepdims=True)
        variance = jnp.mean(centered * centered, axis=1, keepdims=True)
        inv_std = lax.rsqrt(variance + EPSILON)
        norm_hat = centered * inv_std
        for part in range(parts):
            mixed_ref[part, at, :] = norm_hat[:, part * LANES : (part + 1) * LANES]
        inv_ref[at, :] = jnp.broadcast_to(inv_std, (block, LANES))
        normed_ref[at, :] = (norm_hat * gain_ref[...].reshape(1, -1) + shift_ref[...].reshape(1, -1)).astype(BF16)

    def finish_cells(at, branch, grad_normed):
        gain = gain_ref[...].reshape(1, -1)
        branch = branch + bout_ref[...].reshape(1, -1)
        scaled_branch = scale_ref[...].reshape(1, -1) * branch
        new_ref[at, :] = (state_ref[at, :].astype(F32) + scaled_branch).astype(BF16)
        norm_hat = jnp.concatenate([mixed_ref[part, at, :] for part in range(parts)], axis=1)
        scaled = grad_normed * gain
        inner = (
            scaled
            - jnp.mean(scaled, axis=1, keepdims=True)
            - norm_hat * jnp.mean(scaled * norm_hat, axis=1, keepdims=True)
        )
        inv_std = inv_ref[at, :]
        for part in range(parts):
            lanes = slice(part * LANES, (part + 1) * LANES)
            grad_mixed = inv_std * inner[:, lanes]
            gmix_ref[part, at, :] = grad_mixed
            gch_ref[0:1, lanes] += jnp.sum(grad_mixed, axis=0, keepdims=True)
        gch_ref[1:2, :] += jnp.sum(grad_normed * norm_hat, axis=0, keepdims=True)
        gch_ref[2:3, :] += jnp.sum(grad_normed, axis=0, keepdims=True)
        gch_ref[4:5, :] += jnp.sum(cot_ref[at, :].astype(F32) * branch, axis=0, keepdims=True)

    def exchange_core(h):
        return [
            prepare(
                big.at[h, :, :, :, :, 1 - core], core_in.at[h], core_sem, h,
                member=cross * 2 + 1 - core,
            )
        ]

    def across(source, target, sems, h):
        copies = []
        for k in range(1, spots):
            spot = lax.rem(cross + k, spots)
            copies.append(
                prepare(
                    source.at[h, spot], target.at[h, k - 1], sems, h * (spots - 1) + k - 1,
                    member=spot * 2 + core,
                )
            )
        return copies

    def sideways(source, target, sems, h):
        return [prepare(source.at[h, 1 - odd], target.at[h], sems, h, tile=tile + 1 - 2 * odd)]

    def first_hop(h):
        return across(a_x, b_x, bx_sem, h) + sideways(a_y, b_y, by_sem, h)

    def second_hop(h):
        return sideways(c_y, d_y, dy_sem, h) + across(c_x, d_x, dx_sem, h)

    def spot_of(other):
        place = lax.div(other, 2)
        half = quarter // 2
        outer = jnp.logical_or(place < half, place >= 3 * half)
        at = jnp.where(place < half, place, jnp.where(outer, place - 2 * half, place - half))
        return outer, at

    def third_hop(h, k):
        other = along[k]
        outer, at = spot_of(other)
        return pltpu.make_async_remote_copy(
            src_ref=e_out.at[h, jnp.clip(at, 0, half_per - 1)],
            dst_ref=f_in.at[k],
            send_sem=f_send.at[h, k],
            recv_sem=f_recv.at[k],
            device_id={"tile": other},
            device_id_type=MESH,
        )

    def goes(h, k):
        outer, at = spot_of(along[k])
        return outer if h == 0 else jnp.logical_not(outer)

    def start_first(h):
        for copy in exchange_core(h):
            copy.wait()

        def add(j, carry):
            for y in range(2):
                for x in range(spots):
                    for kind in range(2):
                        value = big[h, kind, j, y, x, core].astype(F32) + core_in[h, kind, j, y, x].astype(F32)
                        if kind == 0:
                            a_x[h, x, j, y] = value.astype(BF16)
                        else:
                            a_y[h, y, j, x] = value.astype(BF16)
            return carry

        lax.fori_loop(0, half_per, add, 0)
        for copy in first_hop(h):
            copy.start()

    def start_second(h):
        for copy in first_hop(h):
            copy.wait()

        def add(j, carry):
            for y in range(2):
                value = a_x[h, cross, j, y].astype(F32)
                for k in range(spots - 1):
                    value = value + b_x[h, k, j, y].astype(F32)
                c_y[h, y, j] = value.astype(BF16)
            for x in range(spots):
                value = a_y[h, odd, j, x].astype(F32) + b_y[h, j, x].astype(F32)
                c_x[h, x, j] = value.astype(BF16)
            return carry

        lax.fori_loop(0, half_per, add, 0)
        for copy in second_hop(h):
            copy.start()

    def start_third(h):
        for copy in second_hop(h):
            copy.wait()

        def add(j, carry):
            value = c_y[h, odd, j].astype(F32) + d_y[h, j].astype(F32)
            e_out[h, j, 0] = value.astype(BF16)
            value = c_x[h, cross, j].astype(F32)
            for k in range(spots - 1):
                value = value + d_x[h, k, j].astype(F32)
            e_out[h, j, 1] = value.astype(BF16)
            return carry

        lax.fori_loop(0, half_per, add, 0)
        for k in range(len(along)):

            @pl.when(goes(h, k))
            def _():
                third_hop(h, k).start()

    def bias_of(h):
        quarters = [bin_ref[pl.ds(k * fourth, fourth)].reshape(1, fourth) for k in ORDER[2 * h : 2 * h + 2]]
        return jnp.concatenate(quarters, axis=1)

    def mlp(h, r):
        at = pl.ds(pl.multiple_of(r * block, block), block)
        if h == 0:
            prepare_cells(at)
        here = slice(h * chunk, (h + 1) * chunk)
        win = win_ref[:, here]
        pre = jnp.dot(normed_ref[at, :], win, preferred_element_type=F32) + bias_of(h)
        square = pre * pre
        tanh_value = jnp.tanh(pre * (GELU_SCALE + (GELU_SCALE * GELU_CUBIC) * square))
        half_tanh = 0.5 * tanh_value
        half = 0.5 + half_tanh
        product = pre * half
        activation = product.astype(BF16)
        slope = half + product * (0.5 - half_tanh) * (
            2.0 * GELU_SCALE + (6.0 * GELU_SCALE * GELU_CUBIC) * square
        )
        grad_pre = gact_ref[at, here] * slope
        grad_low = grad_pre.astype(BF16)
        act_ref[at, here] = activation
        glow_ref[at, here] = grad_low
        gbin_ref[:, here] += jnp.sum(grad_pre, axis=0, keepdims=True)

    def close_cells(r):
        at = pl.ds(pl.multiple_of(r * block, block), block)
        branch = jnp.dot(act_ref[at, :], wout_ref[...], preferred_element_type=F32)
        grad_normed = contract_cols(glow_ref[at, :], win_ref[...])
        finish_cells(at, branch, grad_normed)

    def weights(h):
        for kind, (left, right) in enumerate([(glow_ref, normed_ref), (act_ref, low_ref)]):
            value = contract_rows(left[:, h * chunk : (h + 1) * chunk], right[...])
            for index in range(per * members):
                j, y = index // members // 2, index // members % 2
                x, c = index % members // 2, index % 2
                big[h, kind, j, y, x, c] = value[index * rows : (index + 1) * rows].astype(BF16)
        for copy in exchange_core(h):
            copy.start()

    def inner_step(r, carry):
        mlp(0, r)
        return carry

    def outer_step(r, carry):
        mlp(1, r)

        @pl.when(r == 0)
        def _():
            start_first(0)

        return carry

    def close_step(r, carry):
        close_cells(r)

        @pl.when(r == 0)
        def _():
            start_second(0)
            start_first(1)

        return carry

    lax.fori_loop(0, cells // block, inner_step, 0)
    weights(0)
    lax.fori_loop(0, cells // block, outer_step, 0)
    weights(1)
    lax.fori_loop(0, cells // block, close_step, 0)
    new_copy = pltpu.make_async_copy(new_ref, new_hbm, store_sem.at[0])
    new_copy.start()

    def gcenter(part, row):
        at = pl.ds(pl.multiple_of(row * side, side), side)
        return gmix_ref[part, at, :].astype(BF16).astype(F32)

    place(gpad, side, margin, gcenter)
    swap_halo(
        gpad, side, margin, links_ref, gsend, grecv, ghalo_sem, tiles, lambda: None
    )
    lines = s_pack.shape[1]
    s_pack[...] = jnp.zeros_like(s_pack)
    first = taps * taps
    extra = gbin_ref.shape[1] // width
    for row in range(extra):
        at = first + row
        s_pack[at // lines, pl.ds(at % lines, 1), :] = gbin_ref[:, pl.ds(ORDER.index(row) * width, width)]
    for row in range(5):
        at = first + extra + row
        s_pack[at // lines, pl.ds(at % lines, 1), :] = gch_ref[pl.ds(row, 1), :]

    def emit(part, at, value):
        mixed_ref[part, at, :] = value

    regroup(padded, packed, side, margin)
    regroup(gpad, gpacked, side, margin)
    start_third(0)
    kernel_grad(packed, gpacked, gkern_ref, 0, side, taps)
    kernel_grad(packed, gpacked, gkern_ref, 1, side, taps)
    start_second(1)
    kernel_grad(packed, gpacked, gkern_ref, 2, side, taps)
    for up in range(taps):
        for col in range(taps):
            at = up * taps + col
            line = gkern_ref[col, up : up + 1, :]
            s_pack[at // lines, pl.ds(at % lines, 1), :] = line[:, :width] + line[:, width:]
    s_send[...] = s_pack[...].astype(BF16)
    small = [
        remote(s_send.at[mate], sm_in.at[k], sm_sem, k, member=mate) for k, mate in enumerate(mates)
    ]
    convolve(gpacked, taps_ref, side, taps, emit, 0, 1)
    convolve(gpacked, taps_ref, side, taps, emit, 1, 2)
    for copy in small:
        copy.wait()
    total = s_pack[member]
    for k in range(members - 1):
        total = total + sm_in[k].astype(F32)
    st_out[...] = total.astype(BF16)
    st_in[tile] = total.astype(BF16)
    small = [
        remote(st_out, st_in.at[tile], st_sem, k, tile=peer) for k, peer in enumerate(peers)
    ]
    start_third(1)
    convolve(gpacked, taps_ref, side, taps, emit, 2, 3)
    wait_halo(gsend, grecv, ghalo_sem, tiles)
    take_halo(gpad, side, margin, links_ref, grecv, tiles, flank)
    for part in range(parts):
        lanes = pl.ds(part * LANES, LANES)
        correct(gpad, flank, part, kern_ref, side, taps, True, mixed_ref)

        def close(row, carry):
            at = pl.ds(pl.multiple_of(row * LANES, LANES), LANES)
            sgrad_ref[at, lanes] = (cot_ref[at, lanes].astype(F32) + mixed_ref[part, at, :]).astype(BF16)
            return carry

        lax.fori_loop(0, cells // LANES, close, 0)
    store = pltpu.make_async_copy(sgrad_ref, sgrad_hbm, store_sem.at[1])
    store.start()
    for copy in small:
        copy.wait()
    total = st_in[0].astype(F32)
    for k in range(1, tiles):
        total = total + st_in[k].astype(F32)
    s_own[...] = total
    sout_ref[member] = total
    small = [
        remote(s_own, sout_ref.at[member], sg_sem, k, member=mate) for k, mate in enumerate(mates)
    ]
    for k in range(len(along)):
        third_hop(0, k).wait_recv()
        for h in range(chunks):

            @pl.when(goes(h, k))
            def _():
                third_hop(h, k).wait_send()

    outer, at = spot_of(tile)
    for h in range(chunks):

        @pl.when(outer if h == 0 else jnp.logical_not(outer))
        def _():
            for kind in range(2):
                value = e_out[h, jnp.clip(at, 0, half_per - 1), kind].astype(F32)
                for k in range(len(along)):
                    value = value + f_in[k, kind].astype(F32)
                own[kind] = value.astype(BF16)

    out_ref[member] = own[...]
    back = [
        remote(own, out_ref.at[member], g_sem, k, member=mate) for k, mate in enumerate(mates)
    ]
    for copy in small + back:
        copy.wait()
    new_copy.wait()
    store.wait()


def run_whole(links, state, cot, kern, vectors, w_in, w_out, side, members, tiles, chunk=768, block=512):
    cells, width = state.shape
    hidden = w_in.shape[1]
    taps = kern.shape[0]
    margin = taps // 2
    chunks = 2
    half = tiles // chunks // 2
    spots = members // 2
    rows = hidden // (tiles * members)
    piece = lambda *n: pltpu.VMEM((chunks, *n, rows, width), BF16)
    used = taps * taps + hidden // width + 5
    lines = 16 * (-(-used // (16 * members)))
    others = max(spots - 1, 1)
    parts = width // LANES
    spread = spread_of(side, margin)
    dma = lambda *n: pltpu.SemaphoreType.DMA(n)
    strips = (len(OFFSETS), margin, side, width)
    anywhere = pl.BlockSpec(memory_space=pl.ANY)
    return pl.pallas_call(
        functools.partial(whole_kernel, side, taps, members, tiles, chunk, block),
        in_specs=[smem_spec(), anywhere] + [vmem_spec()] * 7 + [anywhere] * 3,
        out_specs=[anywhere] * 2 + [vmem_spec()] * 2,
        out_shape=[
            jax.ShapeDtypeStruct((cells, width), BF16),
            jax.ShapeDtypeStruct((cells, width), BF16),
            jax.ShapeDtypeStruct((members, 2, rows, width), BF16),
            jax.ShapeDtypeStruct((members, lines, width), F32),
        ],
        scratch_shapes=[
            pltpu.VMEM((parts, spread, LANES), F32),
            pltpu.VMEM((parts, spread, LANES), F32),
            pltpu.VMEM((2, margin, parts, pitch_of(side), LANES), F32),
            pltpu.VMEM((packed_of(side, margin), 8, 2 * width), BF16),
            pltpu.VMEM((packed_of(side, margin), 8, 2 * width), BF16),
            pltpu.VMEM((taps * taps, 8, 2 * width), BF16),
            pltpu.VMEM((taps, 8, 2 * width), F32),
            pltpu.VMEM((parts, cells, LANES), F32),
            pltpu.VMEM((cells, LANES), F32),
            pltpu.VMEM((cells, width), BF16),
            pltpu.VMEM((cells, width), BF16),
            pltpu.VMEM((cells, hidden), BF16),
            pltpu.VMEM((cells, hidden), BF16),
            pltpu.VMEM((cells, hidden), F32),
            pltpu.VMEM((parts, cells, LANES), F32),
            pltpu.VMEM((1, hidden), F32),
            pltpu.VMEM((8, width), F32),
            pltpu.VMEM((cells, width), BF16),
            pltpu.VMEM((cells, width), BF16),
            pltpu.VMEM((width, hidden), BF16),
            pltpu.VMEM((hidden, width), BF16),
            pltpu.VMEM((cells, width), BF16),
            pltpu.VMEM((cells, width), BF16),
            pltpu.VMEM(strips, BF16),
            pltpu.VMEM(strips, BF16),
            pltpu.VMEM(strips, BF16),
            pltpu.VMEM(strips, BF16),
            piece(2, half, 2, spots, 2),
            piece(2, half, 2, spots),
            piece(spots, half, 2),
            piece(others, half, 2),
            piece(spots, half),
            piece(others, half),
            piece(2, half, spots),
            piece(half, spots),
            piece(2, half),
            piece(half),
            piece(half, 2),
            pltpu.VMEM((tiles // 2 - 1, 2, rows, width), BF16),
            pltpu.VMEM((2, rows, width), BF16),
            pltpu.VMEM((members, lines, width), F32),
            pltpu.VMEM((members, lines, width), BF16),
            pltpu.VMEM((members - 1, lines, width), BF16),
            pltpu.VMEM((lines, width), BF16),
            pltpu.VMEM((tiles, lines, width), BF16),
            pltpu.VMEM((lines, width), F32),
            dma(10),
            dma(2, len(OFFSETS)),
            dma(2, len(OFFSETS)),
            dma(2, chunks),
            dma(2, chunks * others),
            dma(2, chunks * others),
            dma(2, chunks),
            dma(2, chunks),
            dma(chunks, tiles // 2 - 1),
            dma(tiles // 2 - 1),
            dma(2, members - 1),
            dma(2, members - 1),
            dma(2, tiles - 1),
            dma(2, members - 1),
            dma(2),
        ],
        compiler_params=remote_params(0),
        name="whole",
    )(links, state, kern, *vectors, cot, w_in, w_out)


def finish_kernel(taps, factor, big_hbm, small_hbm, new_hbm, sgrad_hbm, *rest):
    outs, kept = rest[:7], rest[7:]
    big_ref, small_ref, held, win_ref, wout_ref, kern_ref, bin_ref, ch_ref, in_sem, out_sem, sems = kept
    members, _, rows, width = big_ref.shape
    lines = small_ref.shape[1]
    pieces = held.shape[1]
    size = held.shape[2]
    first_in = [
        pltpu.make_async_copy(source, target, in_sem.at[k])
        for k, (source, target) in enumerate([(big_hbm, big_ref), (small_hbm, small_ref)])
    ]
    inward, outward = [], []
    for k, (source, target) in enumerate([(new_hbm, outs[0]), (sgrad_hbm, outs[1])]):
        for piece in range(pieces):
            at = pl.ds(piece * size, size)
            here = held.at[k, piece]
            inward.append(pltpu.make_async_copy(source.at[at, :], here, sems.at[0, k, piece]))
            outward.append(pltpu.make_async_copy(here, target.at[at, :], sems.at[1, k, piece]))
    last_out = [
        pltpu.make_async_copy(source, target, out_sem.at[k])
        for k, (source, target) in enumerate(
            zip((win_ref, wout_ref, kern_ref, bin_ref, ch_ref), outs[2:])
        )
    ]
    for copy in first_in + inward:
        copy.start()
    first_in[0].wait()
    for m in range(members):
        win_ref[pl.ds(m * rows, rows), :] = big_ref[m, 0].astype(F32) * factor
        wout_ref[pl.ds(m * rows, rows), :] = big_ref[m, 1].astype(F32) * factor
    for copy in last_out[:2]:
        copy.start()
    for come, go in zip(inward, outward):
        come.wait()
        go.start()
    first_in[1].wait()

    def line(at):
        return small_ref[at // lines, pl.ds(at % lines, 1), :] * factor

    for at in range(taps * taps):
        kern_ref[at // taps, pl.ds(at % taps, 1), :] = line(at)
    first = taps * taps
    extra = bin_ref.shape[0] // width
    for at in range(extra):
        bin_ref[pl.ds(at * width, width)] = line(first + at).reshape(width)
    for at in range(5):
        ch_ref[pl.ds(at, 1), :] = line(first + extra + at)
    for copy in last_out[2:]:
        copy.start()
    for copy in outward + last_out:
        copy.wait()


def finish(big, small, new, sgrad, share, taps, hidden, factor, pieces=2):
    width = big.shape[3]
    shapes = [(share, width), (share, width), (taps, taps, width), (hidden,), (5, width)]
    anywhere = pl.BlockSpec(memory_space=pl.ANY)
    return pl.pallas_call(
        functools.partial(finish_kernel, taps, factor),
        in_specs=[anywhere] * 4,
        out_specs=[anywhere] * 7,
        out_shape=[jax.ShapeDtypeStruct(new.shape, BF16)] * 2
        + [jax.ShapeDtypeStruct(shape, F32) for shape in shapes],
        scratch_shapes=[
            pltpu.VMEM(big.shape, BF16),
            pltpu.VMEM(small.shape, F32),
            pltpu.VMEM((2, pieces, new.shape[0] // pieces, width), BF16),
        ]
        + [pltpu.VMEM(shape, F32) for shape in shapes]
        + [
            pltpu.SemaphoreType.DMA((2,)),
            pltpu.SemaphoreType.DMA((5,)),
            pltpu.SemaphoreType.DMA((2, 2, pieces)),
        ],
        compiler_params=local_params(),
        name="finish",
    )(big, small, new, sgrad)


def body(
    state,
    cotangent,
    neighbors,
    kernel,
    conv_bias,
    norm_gain,
    norm_shift,
    w_in,
    bias_in,
    w_out,
    bias_out,
    layer_scale,
):
    side, width = state.shape[2], state.shape[4]
    cells = side * side
    center = state.reshape(cells, width)
    cot = cotangent.reshape(cells, width)
    hidden = w_in.shape[1]
    taps = kernel.shape[0]
    tiles = lax.axis_size("tile")
    members = lax.axis_size("member")
    vectors = (conv_bias, norm_gain, norm_shift, bias_in, bias_out, layer_scale)
    new_tile, state_grad, big, small = run_whole(
        neighbors, center, cot, kernel, vectors, w_in, w_out, side, members, tiles
    )
    share = hidden // tiles
    factor = 1.0 / math.sqrt(members * tiles * cells)
    new_tile, state_grad, win_share, *shares = finish(
        big, small, new_tile, state_grad, share, taps, hidden, factor
    )
    return (
        new_tile.reshape(state.shape),
        state_grad.reshape(state.shape),
        win_share.T,
        *shares,
    )


def solution(mesh):
    tiled = P("member", "tile", None, None, None)
    in_specs = (tiled, tiled) + (P(),) * 10
    out_specs = (tiled, tiled, P(None, "tile"), P("tile", None), P(), P(), P())
    return jax.shard_map(body, mesh=mesh, in_specs=in_specs, out_specs=out_specs, check_vma=False)
```
